512 devices in a mesh: col: 64 (over z, x), row: 8 (over y, core).
Axes of the slice: x: 4, y: 4, z: 16, core: 2. Of those that a mesh axis runs over, the one named last changes fastest.
Arguments:
- features: bfloat16 [64, 524288], P(None, ('col', 'row')), may hold values from -6 to 6
- preact: bfloat16 [64, 524288], P(None, ('col', 'row')), may hold values from -8 to 8
- coarse_grad: bfloat16 [128, 65536], P(None, ('col', 'row')), may hold values from -6 to 6
- kernel_one: bfloat16 [27, 64, 64], replicated, may hold values from -0.15625 to 0.15625
- kernel_two: bfloat16 [8, 128, 64], replicated, may hold values from -0.25 to 0.25
- neighbours: int32 [27, 524288], P(None, ('col', 'row')), may hold values from 0 to 3040, as said below
- send_list: int32 [114688], P(('col', 'row')), may hold values from 0 to 1023, as said below
- parent_slot: int32 [524288], P(('col', 'row')), may hold values from 0 to 127, as said below
- child_pos: int32 [524288], P(('col', 'row')), may hold values from 0 to 7, as said below
Outputs:
- feature_grad: bfloat16 [64, 524288], P(None, ('col', 'row'))
- kernel_one_grad: float32 [27, 64, 64], replicated
- kernel_two_grad: float32 [8, 128, 64], replicated
The draws below stay inside these ranges and needn't reach their ends.
Inputs may be any that keep to these rules, and one draw needn't show every extreme that they name: Entries come from the geometry of occupied fine voxels in 16 x 16 x (256) columns, one column a device: neighbour relations are mutual (N(i, o) = j exactly when N(j, 26 - o) = i), entries of 3040 mark empty neighbours, and remote entries only name devices beside the holder along col and row. `send_list`: distinct voxels of the holding device, exactly those that lie on the outermost fine layer of its column along x or y. `parent_slot`: the coarse level is spread over col by a load hash: every value names the parent of exactly 8 fine voxels of the device, so each device along col owns 2 parents of each device of the same row index. `child_pos`: the 8 children of a parent have distinct positions.
All inputs are finite; a program needn't handle non-finite values.
Results may differ from the reference program's by a relative error of at most 0.0049.
Values may be sent and summed in bfloat16 or wider, within the bound.
No kernel may reach another device: no remote copies, remote signals or barrier semaphores. Data moves between devices by JAX's collectives and lax.ppermute only.
A program may use at most 64 MiB of HBM per device.

```python
import jax
import jax.numpy as jnp
import numpy as np
from jax import lax

C1 = 64
C2 = 128
PARENTS = 128
QZ = 128
SITES = 1024
BSIDE = 32
BCORN = 16
HCAP = 224
PCAP = 2
SITES_ALL = 524288
N_COL = 64
N_ROW = 8


def layout_tables():
    cells = np.arange(64)
    across = cells // 8
    along = cells % 8
    rim_x = (across == 0) | (across == 7)
    rim_y = (along == 0) | (along == 7)
    corner = rim_x & rim_y
    side = (rim_x | rim_y) & ~corner
    inner = ~(rim_x | rim_y)
    return (cells[side].astype(np.int32), cells[corner].astype(np.int32), cells[inner].astype(np.int32))


def device_plan(dev_key):
    keys = jax.random.split(dev_key, 5)
    side_cells, corner_cells, inner_cells = layout_tables()
    inner_count = PARENTS - BSIDE - BCORN
    side_pick = jax.random.permutation(keys[0], side_cells.shape[0] * QZ)[:BSIDE].astype(jnp.int32)
    corner_pick = jax.random.permutation(keys[1], corner_cells.shape[0] * QZ)[:BCORN].astype(jnp.int32)
    inner_pick = jax.random.permutation(keys[2], inner_cells.shape[0] * QZ)[:inner_count].astype(jnp.int32)
    cell = jnp.concatenate([jnp.asarray(side_cells)[side_pick // QZ], jnp.asarray(corner_cells)[corner_pick // QZ], jnp.asarray(inner_cells)[inner_pick // QZ]])
    height = jnp.concatenate([side_pick % QZ, corner_pick % QZ, inner_pick % QZ])
    slot_ids = jnp.arange(SITES, dtype=jnp.int32)
    slot_cell = cell[slot_ids // 8]
    slot_child = slot_ids % 8
    local_x = 2 * (slot_cell // 8) + slot_child // 4
    local_y = 2 * (slot_cell % 8) + slot_child // 2 % 2
    outer = (local_x == 0) | (local_x == 15) | (local_y == 0) | (local_y == 15)
    rank_key = jnp.where(outer, 0, SITES).astype(jnp.int32) + slot_ids
    slot_perm = jnp.argsort(rank_key, stable=True).astype(jnp.int32)
    shuffled = jax.random.permutation(keys[3], SITES).astype(jnp.int32)
    voxel_of_rank = ((shuffled - shuffled[0] + SITES - 1) % SITES).astype(jnp.int32)
    order = jnp.zeros((SITES,), jnp.int32).at[voxel_of_rank].set(slot_perm)
    rank_of = jnp.zeros((SITES,), jnp.int32).at[voxel_of_rank].set(slot_ids)
    owner_slot = jax.random.permutation(keys[4], PARENTS).astype(jnp.int32)
    return (cell, height, order, rank_of, voxel_of_rank[:HCAP], owner_slot)


def world_plan(key):
    base = jax.random.fold_in(key, 7301)
    devices = N_COL * N_ROW
    cell, height, order, rank_of, offered, owner_slot = jax.vmap(device_plan)(jax.random.split(base, devices))
    parent = order // 8
    child = order % 8
    dev_ids = jnp.arange(devices, dtype=jnp.int32)[:, None]
    pcell = jnp.take_along_axis(cell, parent, axis=1)
    pheight = jnp.take_along_axis(height, parent, axis=1)
    fine_x = dev_ids // N_ROW * 16 + 2 * (pcell // 8) + child // 4
    fine_y = dev_ids % N_ROW * 16 + 2 * (pcell % 8) + child // 2 % 2
    fine_z = 2 * pheight + child % 2
    size_x = 16 * N_COL
    size_y = 16 * N_ROW
    size_z = 2 * QZ
    ident = dev_ids * SITES + jnp.arange(SITES, dtype=jnp.int32)[None, :]
    grid = jnp.full((size_x, size_y, size_z), -1, jnp.int32).at[fine_x, fine_y, fine_z].set(ident)
    flat_rank = rank_of.reshape(-1)
    sentinel = SITES + 9 * HCAP
    rows_out = []
    for step_x in (-1, 0, 1):
        for step_y in (-1, 0, 1):
            for step_z in (-1, 0, 1):
                near_x = fine_x + step_x
                near_y = fine_y + step_y
                near_z = fine_z + step_z
                inside = (near_x >= 0) & (near_x < size_x) & (near_y >= 0) & (near_y < size_y) & (near_z >= 0) & (near_z < size_z)
                found = grid[jnp.clip(near_x, 0, size_x - 1), jnp.clip(near_y, 0, size_y - 1), jnp.clip(near_z, 0, size_z - 1)]
                found = jnp.where(inside, found, -1)
                safe = jnp.maximum(found, 0)
                near_dev = safe // SITES
                near_site = safe % SITES
                move_col = near_dev // N_ROW - dev_ids // N_ROW
                move_row = near_dev % N_ROW - dev_ids % N_ROW
                remote = SITES + ((move_col + 1) * 3 + move_row + 1) * HCAP + flat_rank[safe]
                entry = jnp.where(found < 0, sentinel, jnp.where(near_dev == dev_ids, near_site, remote))
                rows_out.append(entry.reshape(-1).astype(jnp.int32))
    neighbours = jnp.stack(rows_out)
    send = offered.reshape(-1).astype(jnp.int32)
    slots = jnp.take_along_axis(owner_slot, parent, axis=1).reshape(-1)
    return (neighbours, send, slots, child.reshape(-1).astype(jnp.int32))


def draw_neighbours(key, part):
    return world_plan(key)[0]


def draw_send_list(key, part):
    return world_plan(key)[1]


def draw_parent_slot(key, part):
    return world_plan(key)[2]


def draw_child_pos(key, part):
    return world_plan(key)[3]


def level_of(rng, dims, cuts, least, high):
    def one(axis_at, shards_of):
        steps = jax.random.uniform(jax.random.fold_in(jax.random.fold_in(rng, 6), axis_at), (shards_of,), jnp.float32, least / len(cuts), high / len(cuts))
        return jnp.repeat(jnp.exp(steps), dims[axis_at] // shards_of).reshape((-1,) + (1,) * (len(dims) - axis_at - 1))

    gain = one(*cuts[0])
    for cut in cuts[1:]:
        gain = gain * one(*cut)
    return gain


def noise(stream_key, shape, deviation, limit, cuts=(), held_as=jnp.bfloat16):
    values = jax.random.normal(stream_key, shape, jnp.float32) * deviation
    if len(cuts) > 0:
        values = level_of(stream_key, shape, cuts, -0.22, 0.18) * values
    return jnp.clip(values, min=-limit, max=limit).astype(held_as)


def setup_inputs(seed: int = 0) -> dict:
    arg_keys = jax.random.split(jax.random.key(seed), 10)
    return {
        "features": noise(arg_keys[0], (C1, SITES_ALL), 1.0, 6.0, ((1, 512),)),
        "preact": noise(arg_keys[1], (C1, SITES_ALL), 1.5, 8.0, ((1, 512),)),
        "coarse_grad": noise(arg_keys[2], (C2, PARENTS * N_COL * N_ROW), 1.0, 6.0, ((1, 512),)),
        "kernel_one": noise(arg_keys[3], (27, C1, C1), (27 * C1) ** -0.5, 0.15625),
        "kernel_two": noise(arg_keys[4], (8, C2, C1), (8 * C1) ** -0.5, 0.25),
        "neighbours": draw_neighbours(jax.random.fold_in(arg_keys[9], 71), 0),
        "send_list": draw_send_list(jax.random.fold_in(arg_keys[9], 71), 0),
        "parent_slot": draw_parent_slot(jax.random.fold_in(arg_keys[9], 71), 0),
        "child_pos": draw_child_pos(jax.random.fold_in(arg_keys[9], 71), 0),
    }


def reference(features, preact, coarse_grad, kernel_one, kernel_two, neighbours, send_list, parent_slot, child_pos):
    all_sites = SITES * N_COL * N_ROW
    device = jnp.arange(all_sites, dtype=jnp.int32) // SITES
    dev_col = device // N_ROW
    dev_row = device % N_ROW
    owner = parent_slot // PCAP
    spot = parent_slot % PCAP
    coarse_index = ((owner * N_ROW + dev_row) * PARENTS + dev_col * PCAP + spot).astype(jnp.int32)
    parent_grad = jnp.take(coarse_grad, coarse_index, axis=1)
    pre = preact.astype(jnp.float32)
    gate_sig = jax.nn.sigmoid(pre)
    act = (pre * gate_sig).astype(jnp.bfloat16)

    def per_child(carry, pieces):
        weight, which = pieces
        picked = child_pos == which
        product = jnp.dot(weight.T, parent_grad, preferred_element_type=jnp.float32)
        carry = carry + jnp.where(picked[None, :], product, 0.0)
        masked = jnp.where(picked[None, :], act, jnp.zeros_like(act))
        grad_w = jnp.dot(parent_grad, masked.T, preferred_element_type=jnp.float32)
        return carry, grad_w

    act_grad, two_sum = lax.scan(per_child, jnp.zeros((C1, all_sites), jnp.float32),
                                 (kernel_two, jnp.arange(8, dtype=jnp.int32)))
    pre_grad = (act_grad * gate_sig * (1.0 + pre * (1.0 - gate_sig))).astype(jnp.bfloat16)

    rel = neighbours - SITES
    group = jnp.clip(rel // HCAP, 0, 8)
    place = jnp.clip(rel % HCAP, 0, HCAP - 1)
    near_col = jnp.clip(dev_col[None, :] + group // 3 - 1, 0, N_COL - 1)
    near_row = jnp.clip(dev_row[None, :] + group % 3 - 1, 0, N_ROW - 1)
    other = near_col * N_ROW + near_row
    remote = other * SITES + jnp.take(send_list, other * HCAP + place)
    local = device[None, :] * SITES + neighbours
    glob = jnp.where(neighbours < SITES, local,
                     jnp.where(neighbours < SITES + 9 * HCAP, remote, all_sites)).astype(jnp.int32)
    feat_table = jnp.concatenate([features, jnp.zeros((C1, 1), jnp.bfloat16)], axis=1)
    grad_table = jnp.concatenate([pre_grad, jnp.zeros((C1, 1), jnp.bfloat16)], axis=1)

    def per_offset(carry, pieces):
        near, mirror, weight = pieces
        near_feat = jnp.take(feat_table, near, axis=1)
        grad_w = jnp.dot(pre_grad, near_feat.T, preferred_element_type=jnp.float32)
        near_grad = jnp.take(grad_table, mirror, axis=1)
        carry = carry + jnp.dot(weight.T, near_grad, preferred_element_type=jnp.float32)
        return carry, grad_w

    feat_grad, one_sum = lax.scan(per_offset, jnp.zeros((C1, all_sites), jnp.float32),
                                  (glob, glob[::-1], kernel_one))
    scale = float(all_sites) ** -0.5
    return feat_grad.astype(jnp.bfloat16), one_sum * scale, two_sum * scale
```

```python
import jax
import jax.numpy as jnp
from jax import lax
from jax.experimental import pallas as pl
from jax.experimental.pallas import tpu as pltpu
from jax.sharding import PartitionSpec as P


AXES = ("col", "row")
BF = jnp.bfloat16
F32 = jnp.float32
I32 = jnp.int32
NT = (((1,), (1,)), ((), ()))
NN = (((1,), (0,)), ((), ()))
OUTER = 256
ROWS = 1536
XDIM = 4


def dot(a, b, dims=NN):
    return lax.dot_general(a, b, dims, preferred_element_type=F32)


def onehot(count, width, index, start=0):
    return jnp.where(lax.broadcasted_iota(I32, (count, width), 0) + start == index, 1.0, 0.0).astype(BF)


def call(kernel, outs, args, flops=0, name=None):
    nbytes = sum(a.size * a.dtype.itemsize for a in args) + sum(o.size * o.dtype.itemsize for o in outs)
    return pl.pallas_call(
        kernel,
        out_shape=tuple(outs),
        in_specs=[pl.BlockSpec(memory_space=pltpu.VMEM)] * len(args),
        out_specs=tuple(pl.BlockSpec(memory_space=pltpu.VMEM) for _ in outs),
        cost_estimate=pl.CostEstimate(flops=flops, bytes_accessed=nbytes, transcendentals=0),
        name=name,
    )(*args)


def shape(dims, dtype):
    return jax.ShapeDtypeStruct(dims, dtype)


def pack_kernel(grad_ref, out_ref):
    half = out_ref.shape[0]
    slots = grad_ref.shape[1]
    row = lax.broadcasted_iota(I32, (half, slots), 0)
    col = lax.broadcasted_iota(I32, (half, slots), 1)
    width = grad_ref.shape[0]
    each = out_ref.shape[1] // width
    for side in range(each):
        pick = jnp.where(col == each * row + side, 1.0, 0.0).astype(BF)
        out_ref[:, side * width : (side + 1) * width] = dot(pick, grad_ref[...], NT).astype(BF)


def outer_kernel(feat_ref, near_ref, send_ref, out_ref, near_out_ref):
    sites = feat_ref.shape[1]
    pick = onehot(sites, OUTER, send_ref[...])
    out_ref[...] = dot(feat_ref[...], pick).astype(BF)
    near = near_ref[...]
    high = dot((near // 64).astype(BF), pick)
    low = dot((near % 64).astype(BF), pick)
    near_out_ref[...] = (high * 64.0 + low).astype(I32)


def sorted_kernel(pre_ref, slot_ref, act_ref, slope_ref):
    sites = pre_ref.shape[1]
    blocks = act_ref.shape[0] // pre_ref.shape[0]
    part = sites // blocks
    place = onehot(sites, sites, slot_ref[...])
    pre = dot(pre_ref[...], place, NT)
    gate = 1.0 / (1.0 + jnp.exp(-pre))
    act = (pre * gate).astype(BF)
    slope = gate * (1.0 + pre * (1.0 - gate))
    rows = pre_ref.shape[0]
    for k in range(blocks):
        act_ref[k * rows : (k + 1) * rows, :] = act[:, k * part : (k + 1) * part]
        slope_ref[k * rows : (k + 1) * rows, :] = slope[:, k * part : (k + 1) * part]


def near_kernel(feat_ref, near_ref, out_ref):
    rows, sites = feat_ref.shape
    count = near_ref.shape[0]

    def step(o, carry):
        pick = onehot(sites, sites, near_ref[pl.ds(o, 1), :])
        out_ref[pl.ds(pl.multiple_of(o * rows, rows), rows), :] = dot(feat_ref[...], pick).astype(BF)
        return carry

    lax.fori_loop(0, count, step, 0)
    out_ref[count * rows :, :] = jnp.zeros((out_ref.shape[0] - count * rows, sites), BF)


def beside(near, offset, sites, held, refs, rows):
    dx, dy = offset // 9 - 1, offset // 3 % 3 - 1
    total = None
    for mx in sorted({0, dx}):
        for my in sorted({0, dy}):
            if mx == 0 and my == 0:
                continue
            group = (mx + 1) * 3 + my + 1
            pick = onehot(OUTER, OUTER, near, sites + group * held)
            part = dot(refs[my + 1][(mx + 1) * rows : (mx + 2) * rows, :], pick)
            total = part if total is None else total + part
    return total


def far_kernel(low_ref, mid_ref, high_ref, near_ref, out_ref, *, sites, held, rows):
    refs = (low_ref, mid_ref, high_ref)
    for o in range(near_ref.shape[0]):
        total = beside(near_ref[o : o + 1, :], o, sites, held, refs, rows)
        if total is None:
            total = jnp.zeros((rows, OUTER), F32)
        out_ref[o * rows : (o + 1) * rows, :] = total.astype(BF)
    done = near_ref.shape[0] * rows
    out_ref[done:, :] = jnp.zeros((out_ref.shape[0] - done, OUTER), BF)


def grad_kernel(
    coarse_ref, two_ref, act_ref, slope_ref, slot_ref, send_ref, near_ref, far_ref, sums_ref, pre_ref, pre_out_ref
):
    rows, sites = pre_ref.shape
    width = two_ref.shape[1]
    coarse = jnp.concatenate(
        [coarse_ref[:, k : k + width] for k in range(0, coarse_ref.shape[1], width)], axis=0
    )
    act_grad = dot(two_ref[...], coarse, NT)
    sorted_pre = (act_grad * slope_ref[...]).astype(BF)
    blocks = act_ref.shape[0] // rows
    sorted_pre = jnp.concatenate([sorted_pre[k * rows : (k + 1) * rows, :] for k in range(blocks)], axis=1)
    pre = dot(sorted_pre, onehot(sites, sites, slot_ref[...])).astype(BF)
    pre_ref[...] = pre
    pre_out = dot(pre, onehot(sites, OUTER, send_ref[...])).astype(BF)
    pre_out_ref[...] = pre_out
    pairs = near_ref.shape[0] // 128
    for p in range(pairs):
        part = dot(pre, near_ref[p * 128 : (p + 1) * 128, :], NT)
        part = part + dot(pre_out, far_ref[p * 128 : (p + 1) * 128, :], NT)
        sums_ref[p * rows : (p + 1) * rows, :] = part.astype(sums_ref.dtype)
    base = pairs * rows
    two = dot(act_ref[...], coarse)
    sums_ref[base : base + two.shape[0], :] = two.astype(sums_ref.dtype)
    base = base + two.shape[0]
    sums_ref[base:, :] = jnp.zeros((sums_ref.shape[0] - base, 128), sums_ref.dtype)


def sum_kernel(parts_ref, out_ref, *, scale):
    total = jnp.sum(parts_ref[...].astype(F32), axis=0)
    if scale is not None:
        total = total * scale
    total = total.astype(out_ref.dtype)
    for k in range(out_ref.shape[0]):
        out_ref[k] = total


def unpack_kernel(sums_ref, one_ref, two_ref):
    rows = one_ref.shape[1]
    count = one_ref.shape[0]
    for o in range(count):
        block = sums_ref[o // 2 * rows : (o // 2 + 1) * rows, :].astype(F32)
        one_ref[o] = block[:, (o % 2) * rows : (o % 2 + 1) * rows]
    base = (count + 1) // 2 * rows
    for k in range(two_ref.shape[0]):
        block = sums_ref[base + k * rows : base + (k + 1) * rows, :].astype(F32)
        two_ref[k] = block.T


def local_kernel(pre_ref, near_ref, weight_ref, out_ref):
    rows, sites = pre_ref.shape
    out_ref[...] = jnp.zeros_like(out_ref)

    def step(g, carry):
        parts = []
        for s in range(3):
            pick = onehot(sites, sites, near_ref[pl.ds(g * 3 + s, 1), :])
            parts.append(dot(pre_ref[...], pick).astype(BF))
        out_ref[...] += dot(weight_ref[g], jnp.concatenate(parts, axis=0))
        return carry

    lax.fori_loop(0, near_ref.shape[0] // 3, step, 0)


def finish_kernel(
    local_ref, low_ref, mid_ref, high_ref, near_ref, weight_ref, send_ref, out_ref, *, held
):
    rows, sites = local_ref.shape
    refs = (low_ref, mid_ref, high_ref)
    total = jnp.zeros((rows, OUTER), F32)
    for g in range(near_ref.shape[0] // 3):
        parts = [beside(near_ref[o : o + 1, :], o, sites, held, refs, rows) for o in range(3 * g, 3 * g + 3)]
        if parts[0] is None:
            continue
        total = total + dot(weight_ref[g], jnp.concatenate([p.astype(BF) for p in parts], axis=0))
    first = total.astype(BF)
    rest = total - first.astype(F32)
    second = rest.astype(BF)
    third = (rest - second.astype(F32)).astype(BF)
    spread = dot(jnp.concatenate([first, second, third], axis=0), onehot(sites, OUTER, send_ref[...]), NT)
    spread = spread[:rows] + spread[rows : 2 * rows] + spread[2 * rows :]
    out_ref[...] = (local_ref[...] + spread).astype(BF)


def shift(block, axis, step):
    count = lax.axis_size(axis)
    return lax.ppermute(block, axis, [(i, i + step) for i in range(count) if 0 <= i + step < count])


def around(block):
    three = jnp.concatenate([shift(block, "col", 1), block, shift(block, "col", -1)], axis=0)
    return shift(three, "row", 1), three, shift(three, "row", -1)


def body(
    features, preact, coarse_grad, kernel_one, kernel_two, neighbours, send_list, parent_slot, child_pos
):
    rows, sites = features.shape
    count = neighbours.shape[0]
    wide, owned = coarse_grad.shape
    children = kernel_two.shape[0]
    held = send_list.shape[0]
    n_col, n_row = lax.axis_size("col"), lax.axis_size("row")
    each = owned // n_col
    peers = XDIM * n_row
    layers = n_col * n_row // peers
    plane = [[z * peers + i for i in range(peers)] for z in range(layers)]
    tower = [[z * peers + i for z in range(layers)] for i in range(peers)]

    (packed,) = call(pack_kernel, [shape((n_col, each * wide), BF)], [coarse_grad], name="pack")
    coarse = lax.all_to_all(packed, "col", 0, 0, tiled=True)

    send = jnp.concatenate([send_list, jnp.full((OUTER - held,), -1, I32)])[None, :]
    parent = parent_slot % each * n_col + parent_slot // each
    slot = (child_pos * owned + parent)[None, :]
    two_rows = kernel_two.transpose(0, 2, 1).reshape(children * rows, wide)
    weight = kernel_one[::-1].reshape(count // 3, 3, rows, rows).transpose(0, 3, 1, 2).reshape(count // 3, rows, 3 * rows)

    feat_out, near_out = call(
        outer_kernel,
        [shape((rows, OUTER), BF), shape((count, OUTER), I32)],
        [features, neighbours, send],
        flops=2 * sites * OUTER * 128,
        name="outer",
    )
    feat_low, feat_mid, feat_high = around(feat_out)
    (near,) = call(
        near_kernel,
        [shape(((count + 1) * rows, sites), BF)],
        [features, neighbours],
        flops=2 * 256 * sites * sites * count,
        name="near",
    )
    act, slope = call(
        sorted_kernel,
        [shape((children * rows, owned), BF), shape((children * rows, owned), F32)],
        [preact, slot],
        flops=2 * 256 * sites * sites,
        name="sort",
    )

    def far_body(*refs):
        far_kernel(*refs, sites=sites, held=held, rows=rows)

    (far,) = call(
        far_body,
        [shape(((count + 1) * rows, OUTER), BF)],
        [feat_low, feat_mid, feat_high, near_out],
        flops=2 * 256 * OUTER * OUTER * 48,
        name="far",
    )
    sums, pre_grad, pre_out = call(
        grad_kernel,
        [shape((ROWS, 128), BF), shape((rows, sites), BF), shape((rows, OUTER), BF)],
        [coarse, two_rows, act, slope, slot, send, near, far],
        flops=2 * 256 * sites * (sites + 1792),
        name="grads",
    )

    share = ROWS // peers
    parts = lax.all_to_all(sums.reshape(peers, share, 128), AXES, 0, 0, axis_index_groups=plane, tiled=True)

    def plane_sum(parts_ref, out_ref):
        sum_kernel(parts_ref, out_ref, scale=None)

    (partial,) = call(plane_sum, [shape((layers, share, 128), BF)], [parts], name="plane_sum")
    parts = lax.all_to_all(partial, AXES, 0, 0, axis_index_groups=tower, tiled=True)
    scale = float(sites * n_col * n_row) ** (-0.5)

    def tower_sum(parts_ref, out_ref):
        sum_kernel(parts_ref, out_ref, scale=scale)

    (whole,) = call(tower_sum, [shape((peers, share, 128), BF)], [parts], name="tower_sum")
    whole = lax.all_to_all(whole, AXES, 0, 0, axis_index_groups=plane, tiled=True)
    one_grad, two_grad = call(
        unpack_kernel,
        [shape((count, rows, rows), F32), shape((children, wide, rows), F32)],
        [whole.reshape(ROWS, 128)],
        name="unpack",
    )

    pre_low, pre_mid, pre_high = around(pre_out)
    (local,) = call(
        local_kernel,
        [shape((rows, sites), F32)],
        [pre_grad, neighbours, weight],
        flops=2 * 256 * sites * sites * count,
        name="local",
    )

    def finish(*refs):
        finish_kernel(*refs, held=held)

    (feature_grad,) = call(
        finish,
        [shape((rows, sites), BF)],
        [local, pre_low, pre_mid, pre_high, near_out, weight, send],
        flops=2 * 256 * OUTER * OUTER * 60,
        name="finish",
    )
    return feature_grad, one_grad, two_grad


def solution(mesh):
    placed = (
        P(None, AXES),
        P(None, AXES),
        P(None, AXES),
        P(),
        P(),
        P(None, AXES),
        P(AXES),
        P(AXES),
        P(AXES),
    )
    return jax.shard_map(
        body,
        mesh=mesh,
        in_specs=placed,
        out_specs=(P(None, AXES), P(), P()),
        check_vma=False,
    )
```

```python
import jax
import jax.numpy as jnp
from jax import lax
from jax.experimental import pallas as pl
from jax.experimental.pallas import tpu as pltpu
from jax.sharding import PartitionSpec as P


AXES = ("col", "row")
BF = jnp.bfloat16
F32 = jnp.float32
I32 = jnp.int32
NT = (((1,), (1,)), ((), ()))
NN = (((1,), (0,)), ((), ()))
TN = (((0,), (0,)), ((), ()))
OUTER = 256
ROWS = 1536
XDIM = 4
TILE = 256


def dot(a, b, dims=NN):
    return lax.dot_general(a, b, dims, preferred_element_type=F32)


def onehot(count, width, index, start=0):
    return jnp.where(lax.broadcasted_iota(I32, (count, width), 0) == index - start, 1.0, 0.0).astype(BF)


def call(kernel, outs, args, flops=0, name=None, vmem=16):
    nbytes = sum(a.size * a.dtype.itemsize for a in args) + sum(o.size * o.dtype.itemsize for o in outs)
    return pl.pallas_call(
        kernel,
        out_shape=tuple(outs),
        in_specs=[pl.BlockSpec(memory_space=pltpu.VMEM)] * len(args),
        out_specs=tuple(pl.BlockSpec(memory_space=pltpu.VMEM) for _ in outs),
        cost_estimate=pl.CostEstimate(flops=flops, bytes_accessed=nbytes, transcendentals=0),
        compiler_params=pltpu.CompilerParams(vmem_limit_bytes=vmem << 20),
        name=name,
    )(*args)


def shape(dims, dtype):
    return jax.ShapeDtypeStruct(dims, dtype)


def pack_kernel(grad_ref, out_ref):
    owned = grad_ref.shape[1]
    same = lax.broadcasted_iota(I32, (owned, owned), 0) == lax.broadcasted_iota(I32, (owned, owned), 1)
    out_ref[...] = dot(jnp.where(same, 1.0, 0.0).astype(BF), grad_ref[...], NT).astype(BF)


def outer_kernel(feat_ref, near_ref, send_ref, out_ref, near_out_ref):
    pick = onehot(feat_ref.shape[1], OUTER, send_ref[...])
    out_ref[...] = dot(feat_ref[...], pick).astype(BF)
    near = near_ref[...]
    high = dot((near // 64).astype(BF), pick)
    low = dot((near % 64).astype(BF), pick)
    near_out_ref[...] = (high * 64.0 + low).astype(I32)


def grad_kernel(
    coarse_ref, two_ref, act_in_ref, parent_ref, child_ref, send_ref, pre_ref, pre_out_ref, two_grad_ref
):
    rows, sites = pre_ref.shape
    children = two_ref.shape[0] // rows
    child = child_ref[...]
    parent_grad = dot(coarse_ref[...], onehot(coarse_ref.shape[0], sites, parent_ref[...]), TN).astype(BF)
    stacked = dot(two_ref[...], parent_grad)
    act_grad = stacked[:rows]
    for k in range(1, children):
        act_grad = jnp.where(child == k, stacked[k * rows : (k + 1) * rows], act_grad)
    value = act_in_ref[...].astype(F32)
    gate = 1.0 / (1.0 + jnp.exp(-value))
    pre = (act_grad * gate * (1.0 + value * (1.0 - gate))).astype(BF)
    pre_ref[...] = pre
    pre_out_ref[...] = dot(pre, onehot(sites, OUTER, send_ref[...])).astype(BF)
    act = (value * gate).astype(BF).astype(F32)
    masked = jnp.concatenate([jnp.where(child == k, act, 0.0).astype(BF) for k in range(children)], axis=0)
    two_grad_ref[...] = dot(masked, parent_grad, NT).astype(BF)


def picked(quarters, index, rows):
    stacked = dot(quarters, onehot(TILE, index.shape[1], index & (TILE - 1)))
    part = index // TILE
    total = jnp.zeros((rows, index.shape[1]), F32)
    for k in range(quarters.shape[0] // rows):
        total = jnp.where(part == k, stacked[k * rows : (k + 1) * rows], total)
    return total.astype(BF)


def local_kernel(pre_ref, feat_ref, near_ref, one_ref, *refs, first, last):
    grads_ref, out_ref = refs[-2:]
    rows, sites = pre_ref.shape
    count = one_ref.shape[0]
    quarters = jnp.concatenate([pre_ref[:, k : k + TILE] for k in range(0, sites, TILE)], axis=0)
    if len(refs) == 3:
        out_ref[...] = refs[0][...]
    else:
        out_ref[...] = jnp.zeros_like(out_ref)

    def step(g, carry):
        parts, weights = [], []
        for s in range(4):
            q = g * 4 + s
            parts.append(picked(quarters, near_ref[pl.ds(q, 1), :], rows))
            weights.append(one_ref[jnp.maximum(count - 1 - q, 0)])
        near = jnp.concatenate(parts, axis=0)
        out_ref[...] += dot(jnp.concatenate(weights, axis=0), near, TN)
        grads = dot(feat_ref[...], near, NT)
        for h in range(2):
            start = pl.multiple_of((2 * (g - first) + h) * rows, rows)
            grads_ref[pl.ds(start, rows), :] = grads[:, h * 128 : (h + 1) * 128]
        return carry

    lax.fori_loop(first, last, step, 0)


def beside(near, offset, sites, held, refs, rows):
    dx, dy = offset // 9 - 1, offset // 3 % 3 - 1
    total = None
    for mx in sorted({0, dx}):
        for my in sorted({0, dy}):
            if mx == 0 and my == 0:
                continue
            group = (mx + 1) * 3 + my + 1
            pick = onehot(OUTER, OUTER, near, sites + group * held)
            part = dot(refs[my + 1][(mx + 1) * rows : (mx + 2) * rows, :], pick)
            total = part if total is None else total + part
    return jnp.zeros((rows, OUTER), F32) if total is None else total


def far_kernel(
    low_ref, mid_ref, high_ref, near_ref, feat_ref, first_ref, second_ref, two_ref, sums_ref, far_ref, *, sites, held
):
    rows = feat_ref.shape[0]
    refs = (low_ref, mid_ref, high_ref)
    count = near_ref.shape[0]
    split = first_ref.shape[0]
    for p in range((count + 1) // 2):
        parts = []
        for q in (2 * p, 2 * p + 1):
            if q < count:
                parts.append(beside(near_ref[q : q + 1, :], q, sites, held, refs, rows).astype(BF))
            else:
                parts.append(jnp.zeros((rows, OUTER), BF))
        both = jnp.concatenate(parts, axis=0)
        far_ref[p * 128 : (p + 1) * 128, :] = both
        start = p * rows
        local = first_ref[start : start + rows, :] if start < split else second_ref[start - split : start - split + rows, :]
        sums_ref[start : start + rows, :] = (local + dot(feat_ref[...], both, NT)).astype(BF)
    base = (count + 1) // 2 * rows
    sums_ref[base : base + two_ref.shape[0], :] = two_ref[...]
    base = base + two_ref.shape[0]
    sums_ref[base:, :] = jnp.zeros((sums_ref.shape[0] - base, 128), BF)


def sum_kernel(parts_ref, out_ref, *, scale):
    total = jnp.sum(parts_ref[...].astype(F32), axis=0)
    if scale is not None:
        total = total * scale
    total = total.astype(out_ref.dtype)
    for k in range(out_ref.shape[0]):
        out_ref[k] = total


def unpack_kernel(sums_ref, one_ref, two_ref):
    count, rows = one_ref.shape[:2]
    for p in range((count + 1) // 2):
        block = sums_ref[p * rows : (p + 1) * rows, :].astype(F32).T
        for h in range(2):
            if 2 * p + h < count:
                one_ref[count - 1 - 2 * p - h] = block[h * rows : (h + 1) * rows, :]
    base = (count + 1) // 2 * rows
    for k in range(two_ref.shape[0]):
        two_ref[k] = sums_ref[base + k * rows : base + (k + 1) * rows, :].astype(F32)


def finish_kernel(local_ref, far_ref, one_ref, send_ref, out_ref):
    rows, sites = local_ref.shape
    count = one_ref.shape[0]
    weights = jnp.concatenate([one_ref[count - 1 - q] for q in range(count)], axis=0)
    total = dot(weights, far_ref[: count * rows, :], TN)
    first = total.astype(BF)
    rest = total - first.astype(F32)
    second = rest.astype(BF)
    third = (rest - second.astype(F32)).astype(BF)
    spread = dot(jnp.concatenate([first, second, third], axis=0), onehot(sites, OUTER, send_ref[...]), NT)
    spread = spread[:rows] + spread[rows : 2 * rows] + spread[2 * rows :]
    out_ref[...] = (local_ref[...] + spread).astype(BF)


def shift(block, axis, step):
    count = lax.axis_size(axis)
    return lax.ppermute(block, axis, [(i, i + step) for i in range(count) if 0 <= i + step < count])


def around(block):
    three = jnp.concatenate([shift(block, "col", 1), block, shift(block, "col", -1)], axis=0)
    return shift(three, "row", 1), three, shift(three, "row", -1)


def body(
    features, preact, coarse_grad, kernel_one, kernel_two, neighbours, send_list, parent_slot, child_pos
):
    rows, sites = features.shape
    count = neighbours.shape[0]
    wide, owned = coarse_grad.shape
    children = kernel_two.shape[0]
    held = send_list.shape[0]
    n_col, n_row = lax.axis_size("col"), lax.axis_size("row")
    peers = XDIM * n_row
    layers = n_col * n_row // peers
    plane = [[z * peers + i for i in range(peers)] for z in range(layers)]
    tower = [[z * peers + i for z in range(layers)] for i in range(peers)]

    (packed,) = call(pack_kernel, [shape((owned, wide), BF)], [coarse_grad], name="pack")
    coarse = lax.all_to_all(packed.reshape(n_col, owned // n_col, wide), "col", 0, 0, tiled=True)
    coarse = coarse.reshape(owned, wide)

    send = jnp.concatenate([send_list, jnp.full((OUTER - held,), -1, I32)])[None, :]
    near = jnp.concatenate([neighbours, jnp.full((1, sites), sites + 9 * held, I32)], axis=0)
    two_rows = kernel_two.transpose(0, 2, 1).reshape(children * rows, wide)
    feat_out, near_out = call(
        outer_kernel,
        [shape((rows, OUTER), BF), shape((count, OUTER), I32)],
        [features, neighbours, send],
        flops=2 * sites * OUTER * 128,
        name="outer",
    )
    pre_grad, pre_out, two_part = call(
        grad_kernel,
        [shape((rows, sites), BF), shape((rows, OUTER), BF), shape((children * rows, wide), BF)],
        [coarse, two_rows, preact, parent_slot[None, :], child_pos[None, :], send],
        flops=2 * 512 * sites * 512,
        name="grads",
    )
    pre_low, pre_mid, pre_high = around(pre_out)

    quads = (count + 3) // 4
    cut = (quads + 1) // 2
    halves, local = [], None
    for first, last in ((0, cut), (cut, quads)):

        def local_body(*refs, first=first, last=last):
            local_kernel(*refs, first=first, last=last)

        part, local = call(
            local_body,
            [shape(((last - first) * 2 * rows, 128), F32), shape((rows, sites), F32)],
            [pre_grad, features, near, kernel_one] + ([] if local is None else [local]),
            flops=2 * 256 * sites * 512 * 4 * (last - first),
            name="local",
        )
        halves.append(part)

    def far_body(*refs):
        far_kernel(*refs, sites=sites, held=held)

    sums, far = call(
        far_body,
        [shape((ROWS, 128), BF), shape(((count + 1) * rows, OUTER), BF)],
        [pre_low, pre_mid, pre_high, near_out, feat_out, *halves, two_part],
        flops=2 * 256 * OUTER * OUTER * 48,
        name="far",
    )

    share = ROWS // peers
    parts = lax.all_to_all(sums.reshape(peers, share, 128), AXES, 0, 0, axis_index_groups=plane, tiled=True)

    def plane_sum(parts_ref, out_ref):
        sum_kernel(parts_ref, out_ref, scale=None)

    (partial,) = call(plane_sum, [shape((layers, share, 128), BF)], [parts], name="plane_sum")
    parts = lax.all_to_all(partial, AXES, 0, 0, axis_index_groups=tower, tiled=True)
    scale = float(sites * n_col * n_row) ** (-0.5)

    def tower_sum(parts_ref, out_ref):
        sum_kernel(parts_ref, out_ref, scale=scale)

    (whole,) = call(tower_sum, [shape((peers, share, 128), BF)], [parts], name="tower_sum")
    whole = lax.all_to_all(whole, AXES, 0, 0, axis_index_groups=plane, tiled=True)
    one_grad, two_grad = call(
        unpack_kernel,
        [shape((count, rows, rows), F32), shape((children, rows, wide), F32)],
        [whole.reshape(ROWS, 128)],
        name="unpack",
    )
    (feature_grad,) = call(
        finish_kernel,
        [shape((rows, sites), BF)],
        [local, far, kernel_one, send],
        flops=2 * 256 * OUTER * sites * 4,
        name="finish",
    )
    return feature_grad, one_grad, two_grad.transpose(0, 2, 1)


def solution(mesh):
    placed = (
        P(None, AXES),
        P(None, AXES),
        P(None, AXES),
        P(),
        P(),
        P(None, AXES),
        P(AXES),
        P(AXES),
        P(AXES),
    )
    return jax.shard_map(
        body,
        mesh=mesh,
        in_specs=placed,
        out_specs=(P(None, AXES), P(), P()),
        check_vma=False,
    )
```

```python
import jax
import jax.numpy as jnp
from jax import lax
from jax.experimental import pallas as pl
from jax.experimental.pallas import tpu as pltpu
from jax.sharding import PartitionSpec as P


AXES = ("col", "row")
BF = jnp.bfloat16
F32 = jnp.float32
I32 = jnp.int32
NT = (((1,), (1,)), ((), ()))
NN = (((1,), (0,)), ((), ()))
TN = (((0,), (0,)), ((), ()))
OUTER = 256
ROWS = 1536
XDIM = 4
TILE = 256


def dot(a, b, dims=NN):
    return lax.dot_general(a, b, dims, preferred_element_type=F32)


def onehot(count, width, index, start=0):
    return jnp.where(lax.broadcasted_iota(I32, (count, width), 0) == index - start, 1.0, 0.0).astype(BF)


def call(kernel, outs, args, flops=0, name=None, vmem=16):
    nbytes = sum(a.size * a.dtype.itemsize for a in args) + sum(o.size * o.dtype.itemsize for o in outs)
    return pl.pallas_call(
        kernel,
        out_shape=tuple(outs),
        in_specs=[pl.BlockSpec(memory_space=pltpu.VMEM)] * len(args),
        out_specs=tuple(pl.BlockSpec(memory_space=pltpu.VMEM) for _ in outs),
        cost_estimate=pl.CostEstimate(flops=flops, bytes_accessed=nbytes, transcendentals=0),
        compiler_params=pltpu.CompilerParams(vmem_limit_bytes=vmem << 20),
        name=name,
    )(*args)


def shape(dims, dtype):
    return jax.ShapeDtypeStruct(dims, dtype)


def pack_kernel(grad_ref, out_ref):
    owned = grad_ref.shape[1]
    same = lax.broadcasted_iota(I32, (owned, owned), 0) == lax.broadcasted_iota(I32, (owned, owned), 1)
    out_ref[...] = dot(jnp.where(same, 1.0, 0.0).astype(BF), grad_ref[...], NT).astype(BF)


def outer_kernel(feat_ref, near_ref, send_ref, out_ref, near_out_ref):
    pick = onehot(feat_ref.shape[1], OUTER, send_ref[...])
    out_ref[...] = dot(feat_ref[...], pick).astype(BF)
    near = near_ref[...]
    high = dot((near // 64).astype(BF), pick)
    low = dot((near % 64).astype(BF), pick)
    near_out_ref[...] = (high * 64.0 + low).astype(I32)


def grad_kernel(
    coarse_ref, two_ref, act_in_ref, parent_ref, child_ref, send_ref, pre_ref, pre_out_ref, two_grad_ref
):
    rows, sites = pre_ref.shape
    children = two_ref.shape[0] // rows
    child = child_ref[...]
    parent_grad = dot(coarse_ref[...], onehot(coarse_ref.shape[0], sites, parent_ref[...]), TN).astype(BF)
    stacked = dot(two_ref[...], parent_grad)
    act_grad = stacked[:rows]
    for k in range(1, children):
        act_grad = jnp.where(child == k, stacked[k * rows : (k + 1) * rows], act_grad)
    value = act_in_ref[...].astype(F32)
    gate = 1.0 / (1.0 + jnp.exp(-value))
    pre = (act_grad * gate * (1.0 + value * (1.0 - gate))).astype(BF)
    pre_ref[...] = pre
    pre_out_ref[...] = dot(pre, onehot(sites, OUTER, send_ref[...])).astype(BF)
    act = (value * gate).astype(BF).astype(F32)
    masked = jnp.concatenate([jnp.where(child == k, act, 0.0).astype(BF) for k in range(children)], axis=0)
    two_grad_ref[...] = dot(masked, parent_grad, NT).astype(BF)


def merged(stacked, part, rows):
    blocks = [stacked[k : k + rows] for k in range(0, stacked.shape[0], rows)]
    bit = 1
    while len(blocks) > 1:
        odd = (part & bit) != 0
        blocks = [jnp.where(odd, blocks[k + 1], blocks[k]) for k in range(0, len(blocks), 2)]
        bit *= 2
    return blocks[0].astype(BF)


def local_kernel(pre_ref, feat_ref, index_ref, grads_ref, near_ref, *, first, last):
    rows, sites = pre_ref.shape
    quarters = jnp.concatenate([pre_ref[:, k : k + TILE] for k in range(0, sites, TILE)], axis=0)

    def step(g, carry):
        parts = []
        for s in range(4):
            index = index_ref[pl.ds(g * 4 + s, 1), :]
            place = jnp.where(index < sites, index & (TILE - 1), -1)
            parts.append(merged(dot(quarters, onehot(TILE, sites, place)), index // TILE, rows))
        near = jnp.concatenate(parts, axis=0)
        near_ref[pl.ds(pl.multiple_of((g - first) * 4 * rows, 4 * rows), 4 * rows), :] = near
        grads = dot(feat_ref[...], near, NT)
        for h in range(2):
            start = pl.multiple_of((2 * (g - first) + h) * rows, rows)
            grads_ref[pl.ds(start, rows), :] = grads[:, h * 128 : (h + 1) * 128]
        return carry

    lax.fori_loop(first, last, step, 0)


def far_kernel(
    low_ref, mid_ref, high_ref, near_ref, feat_ref, first_ref, second_ref, two_ref, sums_ref, far_ref, *, sites, held
):
    rows = feat_ref.shape[0]
    refs = (low_ref, mid_ref, high_ref)
    count = near_ref.shape[0]
    split = first_ref.shape[0]
    group = near_ref[...] - sites
    beside = ((group.astype(F32) + 0.5) * (1.0 / held)).astype(I32)
    place = group - beside * held
    beside = jnp.where(group < 0, -1, beside)
    blocks = []
    for line in range(count // 3):
        dx, dy = line // 3 - 1, line % 3 - 1
        moves = [(mx, my) for mx in sorted({0, dx}) for my in sorted({0, dy}) if (mx, my) != (0, 0)]
        if not moves:
            blocks += [jnp.zeros((rows, OUTER), BF)] * 3
            continue
        tables = jnp.concatenate([refs[my + 1][(mx + 1) * rows : (mx + 2) * rows, :] for mx, my in moves], axis=0)
        lanes = [slice(3 * line + k, 3 * line + k + 1) for k in range(3)]
        index = jnp.concatenate([place[k, :] for k in lanes], axis=1)
        part = jnp.concatenate([beside[k, :] for k in lanes], axis=1)
        stacked = dot(tables, onehot(TILE, 3 * OUTER, index))
        total = jnp.zeros((rows, 3 * OUTER), F32)
        for k, (mx, my) in enumerate(moves):
            total = jnp.where(part == (mx + 1) * 3 + my + 1, stacked[k * rows : (k + 1) * rows], total)
        total = total.astype(BF)
        blocks += [total[:, k * OUTER : (k + 1) * OUTER] for k in range(3)]
    blocks.append(jnp.zeros((rows, OUTER), BF))
    for q, block in enumerate(blocks):
        far_ref[q * rows : (q + 1) * rows, :] = block
    for g in range(len(blocks) // 4):
        both = jnp.concatenate(blocks[4 * g : 4 * g + 4], axis=0)
        grads = dot(feat_ref[...], both, NT)
        for h in range(2):
            start = (2 * g + h) * rows
            local = first_ref[start : start + rows, :] if start < split else second_ref[start - split : start - split + rows, :]
            sums_ref[start : start + rows, :] = (local + grads[:, h * 128 : (h + 1) * 128]).astype(BF)
    base = len(blocks) // 2 * rows
    sums_ref[base : base + two_ref.shape[0], :] = two_ref[...]
    base = base + two_ref.shape[0]
    sums_ref[base:, :] = jnp.zeros((sums_ref.shape[0] - base, 128), BF)


def sum_kernel(parts_ref, out_ref, *, scale):
    total = jnp.sum(parts_ref[...].astype(F32), axis=0)
    if scale is not None:
        total = total * scale
    total = total.astype(out_ref.dtype)
    for k in range(out_ref.shape[0]):
        out_ref[k] = total


def unpack_kernel(sums_ref, one_ref, two_ref):
    count, rows = one_ref.shape[:2]
    for p in range((count + 1) // 2):
        block = sums_ref[p * rows : (p + 1) * rows, :].astype(F32).T
        for h in range(2):
            if 2 * p + h < count:
                one_ref[count - 1 - 2 * p - h] = block[h * rows : (h + 1) * rows, :]
    base = (count + 1) // 2 * rows
    for k in range(two_ref.shape[0]):
        two_ref[k] = sums_ref[base + k * rows : base + (k + 1) * rows, :].astype(F32)


def finish_kernel(first_ref, second_ref, far_ref, one_ref, send_ref, out_ref):
    rows, sites = out_ref.shape
    count = one_ref.shape[0]
    split = first_ref.shape[0]
    weights = jnp.concatenate([one_ref[count - 1 - q] for q in range(count)], axis=0)
    total = dot(weights, far_ref[: count * rows, :], TN)
    first = total.astype(BF)
    rest = total - first.astype(F32)
    second = rest.astype(BF)
    third = (rest - second.astype(F32)).astype(BF)
    spread = dot(jnp.concatenate([first, second, third], axis=0), onehot(sites, OUTER, send_ref[...]), NT)
    spread = spread[:rows] + spread[rows : 2 * rows] + spread[2 * rows :]
    local = dot(weights[:split], first_ref[...], TN)
    local = local + dot(weights[split:], second_ref[: count * rows - split, :], TN)
    out_ref[...] = (local + spread).astype(BF)


def shift(block, axis, step):
    count = lax.axis_size(axis)
    return lax.ppermute(block, axis, [(i, i + step) for i in range(count) if 0 <= i + step < count])


def around(block):
    three = jnp.concatenate([shift(block, "col", 1), block, shift(block, "col", -1)], axis=0)
    return shift(three, "row", 1), three, shift(three, "row", -1)


def body(
    features, preact, coarse_grad, kernel_one, kernel_two, neighbours, send_list, parent_slot, child_pos
):
    rows, sites = features.shape
    count = neighbours.shape[0]
    wide, owned = coarse_grad.shape
    children = kernel_two.shape[0]
    held = send_list.shape[0]
    n_col, n_row = lax.axis_size("col"), lax.axis_size("row")
    peers = XDIM * n_row
    layers = n_col * n_row // peers
    plane = [[z * peers + i for i in range(peers)] for z in range(layers)]
    tower = [[z * peers + i for z in range(layers)] for i in range(peers)]

    (packed,) = call(pack_kernel, [shape((owned, wide), BF)], [coarse_grad], name="pack", vmem=60)
    coarse = lax.all_to_all(packed.reshape(n_col, owned // n_col, wide), "col", 0, 0, tiled=True)
    coarse = coarse.reshape(owned, wide)

    send = jnp.concatenate([send_list, jnp.full((OUTER - held,), -1, I32)])[None, :]
    near = jnp.concatenate([neighbours, jnp.full((1, sites), sites + 9 * held, I32)], axis=0)
    two_rows = kernel_two.transpose(0, 2, 1).reshape(children * rows, wide)
    feat_out, near_out = call(
        outer_kernel,
        [shape((rows, OUTER), BF), shape((count, OUTER), I32)],
        [features, neighbours, send],
        flops=2 * sites * OUTER * 128,
        name="outer",
    )
    pre_grad, pre_out, two_part = call(
        grad_kernel,
        [shape((rows, sites), BF), shape((rows, OUTER), BF), shape((children * rows, wide), BF)],
        [coarse, two_rows, preact, parent_slot[None, :], child_pos[None, :], send],
        flops=2 * 512 * sites * 512,
        name="grads",
    )
    pre_low, pre_mid, pre_high = around(pre_out)

    quads = (count + 3) // 4
    cut = (quads + 1) // 2
    halves, nears = [], []
    for first, last in ((0, cut), (cut, quads)):

        def local_body(*refs, first=first, last=last):
            local_kernel(*refs, first=first, last=last)

        part, block = call(
            local_body,
            [shape(((last - first) * 2 * rows, 128), F32), shape(((last - first) * 4 * rows, sites), BF)],
            [pre_grad, features, near],
            flops=2 * 256 * sites * 512 * 4 * (last - first),
            name="local",
        )
        halves.append(part)
        nears.append(block)

    def far_body(*refs):
        far_kernel(*refs, sites=sites, held=held)

    sums, far = call(
        far_body,
        [shape((ROWS, 128), BF), shape(((count + 1) * rows, OUTER), BF)],
        [pre_low, pre_mid, pre_high, near_out, feat_out, *halves, two_part],
        flops=2 * 256 * OUTER * OUTER * 48,
        name="far",
    )

    share = ROWS // peers
    parts = lax.all_to_all(sums.reshape(peers, share, 128), AXES, 0, 0, axis_index_groups=plane, tiled=True)

    def plane_sum(parts_ref, out_ref):
        sum_kernel(parts_ref, out_ref, scale=None)

    (partial,) = call(plane_sum, [shape((layers, share, 128), BF)], [parts], name="plane_sum")
    parts = lax.all_to_all(partial, AXES, 0, 0, axis_index_groups=tower, tiled=True)
    scale = float(sites * n_col * n_row) ** (-0.5)

    def tower_sum(parts_ref, out_ref):
        sum_kernel(parts_ref, out_ref, scale=scale)

    (whole,) = call(tower_sum, [shape((peers, share, 128), BF)], [parts], name="tower_sum")
    whole = lax.all_to_all(whole, AXES, 0, 0, axis_index_groups=plane, tiled=True)
    one_grad, two_grad = call(
        unpack_kernel,
        [shape((count, rows, rows), F32), shape((children, rows, wide), F32)],
        [whole.reshape(ROWS, 128)],
        name="unpack",
    )
    (feature_grad,) = call(
        finish_kernel,
        [shape((rows, sites), BF)],
        [*nears, far, kernel_one, send],
        flops=2 * 256 * sites * 2048,
        name="finish",
    )
    return feature_grad, one_grad, two_grad.transpose(0, 2, 1)


def solution(mesh):
    placed = (
        P(None, AXES),
        P(None, AXES),
        P(None, AXES),
        P(),
        P(),
        P(None, AXES),
        P(AXES),
        P(AXES),
        P(AXES),
    )
    return jax.shard_map(
        body,
        mesh=mesh,
        in_specs=placed,
        out_specs=(P(None, AXES), P(), P()),
        check_vma=False,
    )
```

```python
import jax
import jax.numpy as jnp
from jax import lax
from jax.experimental import pallas as pl
from jax.experimental.pallas import tpu as pltpu
from jax.sharding import PartitionSpec as P


AXES = ("col", "row")
BF = jnp.bfloat16
F32 = jnp.float32
I32 = jnp.int32
NT = (((1,), (1,)), ((), ()))
NN = (((1,), (0,)), ((), ()))
TN = (((0,), (0,)), ((), ()))
OUTER = 256
ROWS = 1536
XDIM = 8
TILE = 256


def dot(a, b, dims=NN):
    return lax.dot_general(a, b, dims, preferred_element_type=F32)


def onehot(count, width, index, start=0):
    return jnp.where(lax.broadcasted_iota(I32, (count, width), 0) == index - start, 1.0, 0.0).astype(BF)


def call(kernel, outs, args, flops=0, name=None, vmem=16):
    nbytes = sum(a.size * a.dtype.itemsize for a in args) + sum(o.size * o.dtype.itemsize for o in outs)
    return pl.pallas_call(
        kernel,
        out_shape=tuple(outs),
        in_specs=[pl.BlockSpec(memory_space=pltpu.VMEM)] * len(args),
        out_specs=tuple(pl.BlockSpec(memory_space=pltpu.VMEM) for _ in outs),
        cost_estimate=pl.CostEstimate(flops=flops, bytes_accessed=nbytes, transcendentals=0),
        compiler_params=pltpu.CompilerParams(vmem_limit_bytes=vmem << 20),
        name=name,
    )(*args)


def shape(dims, dtype):
    return jax.ShapeDtypeStruct(dims, dtype)


def pack_kernel(grad_ref, out_ref):
    owned = grad_ref.shape[1]
    same = lax.broadcasted_iota(I32, (owned, owned), 0) == lax.broadcasted_iota(I32, (owned, owned), 1)
    out_ref[...] = dot(jnp.where(same, 1.0, 0.0).astype(BF), grad_ref[...], NT).astype(BF)


def outer_kernel(feat_ref, near_ref, send_ref, out_ref, near_out_ref):
    pick = onehot(feat_ref.shape[1], OUTER, send_ref[...])
    out_ref[...] = dot(feat_ref[...], pick).astype(BF)
    near = near_ref[...]
    high = dot((near // 64).astype(BF), pick)
    low = dot((near % 64).astype(BF), pick)
    near_out_ref[...] = (high * 64.0 + low).astype(I32)


def grad_kernel(
    coarse_ref, two_ref, act_in_ref, parent_ref, child_ref, send_ref, pre_ref, pre_out_ref, two_grad_ref
):
    rows, sites = pre_ref.shape
    children = two_ref.shape[0] // rows
    child = child_ref[...]
    parent_grad = dot(coarse_ref[...], onehot(coarse_ref.shape[0], sites, parent_ref[...]), TN).astype(BF)
    stacked = dot(two_ref[...], parent_grad)
    act_grad = stacked[:rows]
    for k in range(1, children):
        act_grad = jnp.where(child == k, stacked[k * rows : (k + 1) * rows], act_grad)
    value = act_in_ref[...].astype(F32)
    gate = 1.0 / (1.0 + jnp.exp(-value))
    pre = (act_grad * gate * (1.0 + value * (1.0 - gate))).astype(BF)
    pre_ref[...] = pre
    pre_out_ref[...] = dot(pre, onehot(sites, OUTER, send_ref[...])).astype(BF)
    act = (value * gate).astype(BF).astype(F32)
    masked = jnp.concatenate([jnp.where(child == k, act, 0.0).astype(BF) for k in range(children)], axis=0)
    two_grad_ref[...] = dot(masked, parent_grad, NT).astype(BF)


def merged(stacked, part, rows):
    blocks = [stacked[k : k + rows] for k in range(0, stacked.shape[0], rows)]
    bit = 1
    while len(blocks) > 1:
        odd = (part & bit) != 0
        blocks = [jnp.where(odd, blocks[k + 1], blocks[k]) for k in range(0, len(blocks), 2)]
        bit *= 2
    return blocks[0].astype(BF)


def local_kernel(pre_ref, feat_ref, index_ref, one_ref, *refs, first, last):
    grads_ref, out_ref = refs[-2:]
    rows, sites = pre_ref.shape
    count = one_ref.shape[0]
    out_ref[...] = refs[0][...] if len(refs) == 3 else jnp.zeros_like(out_ref)
    quarters = jnp.concatenate([pre_ref[:, k : k + TILE] for k in range(0, sites, TILE)], axis=0)

    def step(g, carry):
        parts, weights = [], []
        for s in range(4):
            q = g * 4 + s
            weights.append(one_ref[jnp.maximum(count - 1 - q, 0)])
            index = index_ref[pl.ds(q, 1), :]
            place = jnp.where(index < sites, index & (TILE - 1), -1)
            parts.append(merged(dot(quarters, onehot(TILE, sites, place)), index // TILE, rows))
        near = jnp.concatenate(parts, axis=0)
        out_ref[...] += dot(jnp.concatenate(weights, axis=0), near, TN)
        grads = dot(feat_ref[...], near, NT)
        for h in range(2):
            start = pl.multiple_of((2 * (g - first) + h) * rows, rows)
            grads_ref[pl.ds(start, rows), :] = grads[:, h * 128 : (h + 1) * 128]
        return carry

    lax.fori_loop(first, last, step, 0)


def far_kernel(
    low_ref, mid_ref, high_ref, near_ref, feat_ref, first_ref, second_ref, two_ref, sums_ref, far_ref, *, sites, held
):
    rows = feat_ref.shape[0]
    refs = (low_ref, mid_ref, high_ref)
    count = near_ref.shape[0]
    split = first_ref.shape[0]
    group = near_ref[...] - sites
    beside = ((group.astype(F32) + 0.5) * (1.0 / held)).astype(I32)
    place = group - beside * held
    beside = jnp.where(group < 0, -1, beside)
    blocks = []
    for line in range(count // 3):
        dx, dy = line // 3 - 1, line % 3 - 1
        moves = [(mx, my) for mx in sorted({0, dx}) for my in sorted({0, dy}) if (mx, my) != (0, 0)]
        if not moves:
            blocks += [jnp.zeros((rows, OUTER), BF)] * 3
            continue
        tables = jnp.concatenate([refs[my + 1][(mx + 1) * rows : (mx + 2) * rows, :] for mx, my in moves], axis=0)
        lanes = [slice(3 * line + k, 3 * line + k + 1) for k in range(3)]
        index = jnp.concatenate([place[k, :] for k in lanes], axis=1)
        part = jnp.concatenate([beside[k, :] for k in lanes], axis=1)
        stacked = dot(tables, onehot(TILE, 3 * OUTER, index))
        total = jnp.zeros((rows, 3 * OUTER), F32)
        for k, (mx, my) in enumerate(moves):
            total = jnp.where(part == (mx + 1) * 3 + my + 1, stacked[k * rows : (k + 1) * rows], total)
        total = total.astype(BF)
        blocks += [total[:, k * OUTER : (k + 1) * OUTER] for k in range(3)]
    blocks.append(jnp.zeros((rows, OUTER), BF))
    for q, block in enumerate(blocks):
        far_ref[q * rows : (q + 1) * rows, :] = block
    for g in range(len(blocks) // 4):
        both = jnp.concatenate(blocks[4 * g : 4 * g + 4], axis=0)
        grads = dot(feat_ref[...], both, NT)
        for h in range(2):
            start = (2 * g + h) * rows
            local = first_ref[start : start + rows, :] if start < split else second_ref[start - split : start - split + rows, :]
            sums_ref[start : start + rows, :] = (local + grads[:, h * 128 : (h + 1) * 128]).astype(BF)
    base = len(blocks) // 2 * rows
    sums_ref[base : base + two_ref.shape[0], :] = two_ref[...]
    base = base + two_ref.shape[0]
    sums_ref[base:, :] = jnp.zeros((sums_ref.shape[0] - base, 128), BF)


def sum_kernel(parts_ref, out_ref, *, scale):
    total = jnp.sum(parts_ref[...].astype(F32), axis=0)
    if scale is not None:
        total = total * scale
    total = total.astype(out_ref.dtype)
    for k in range(out_ref.shape[0]):
        out_ref[k] = total


def unpack_kernel(sums_ref, one_ref, two_ref):
    count, rows = one_ref.shape[:2]
    for p in range((count + 1) // 2):
        block = sums_ref[p * rows : (p + 1) * rows, :].astype(F32).T
        for h in range(2):
            if 2 * p + h < count:
                one_ref[count - 1 - 2 * p - h] = block[h * rows : (h + 1) * rows, :]
    base = (count + 1) // 2 * rows
    for k in range(two_ref.shape[0]):
        two_ref[k] = sums_ref[base + k * rows : base + (k + 1) * rows, :].astype(F32)


def finish_kernel(local_ref, far_ref, one_ref, send_ref, out_ref):
    rows, sites = local_ref.shape
    count = one_ref.shape[0]
    weights = jnp.concatenate([one_ref[count - 1 - q] for q in range(count)], axis=0)
    total = dot(weights, far_ref[: count * rows, :], TN)
    first = total.astype(BF)
    rest = total - first.astype(F32)
    second = rest.astype(BF)
    third = (rest - second.astype(F32)).astype(BF)
    spread = dot(jnp.concatenate([first, second, third], axis=0), onehot(sites, OUTER, send_ref[...]), NT)
    spread = spread[:rows] + spread[rows : 2 * rows] + spread[2 * rows :]
    out_ref[...] = (local_ref[...] + spread).astype(BF)


def shift(block, axis, step):
    count = lax.axis_size(axis)
    return lax.ppermute(block, axis, [(i, i + step) for i in range(count) if 0 <= i + step < count])


def around(block):
    three = jnp.concatenate([shift(block, "col", 1), block, shift(block, "col", -1)], axis=0)
    return shift(three, "row", 1), three, shift(three, "row", -1)


def body(
    features, preact, coarse_grad, kernel_one, kernel_two, neighbours, send_list, parent_slot, child_pos
):
    rows, sites = features.shape
    count = neighbours.shape[0]
    wide, owned = coarse_grad.shape
    children = kernel_two.shape[0]
    held = send_list.shape[0]
    n_col, n_row = lax.axis_size("col"), lax.axis_size("row")
    peers = XDIM * n_row
    layers = n_col * n_row // peers
    plane = [[z * peers + i for i in range(peers)] for z in range(layers)]
    tower = [[z * peers + i for z in range(layers)] for i in range(peers)]

    (packed,) = call(pack_kernel, [shape((owned, wide), BF)], [coarse_grad], name="pack")
    coarse = lax.all_to_all(packed.reshape(n_col, owned // n_col, wide), "col", 0, 0, tiled=True)
    coarse = coarse.reshape(owned, wide)

    send = jnp.concatenate([send_list, jnp.full((OUTER - held,), -1, I32)])[None, :]
    near = jnp.concatenate([neighbours, jnp.full((1, sites), sites + 9 * held, I32)], axis=0)
    two_rows = kernel_two.transpose(0, 2, 1).reshape(children * rows, wide)
    feat_out, near_out = call(
        outer_kernel,
        [shape((rows, OUTER), BF), shape((count, OUTER), I32)],
        [features, neighbours, send],
        flops=2 * sites * OUTER * 128,
        name="outer",
    )
    pre_grad, pre_out, two_part = call(
        grad_kernel,
        [shape((rows, sites), BF), shape((rows, OUTER), BF), shape((children * rows, wide), BF)],
        [coarse, two_rows, preact, parent_slot[None, :], child_pos[None, :], send],
        flops=2 * 512 * sites * 512,
        name="grads",
    )
    pre_low, pre_mid, pre_high = around(pre_out)

    quads = (count + 3) // 4
    cut = (quads + 1) // 2
    halves, local = [], None
    for first, last in ((0, cut), (cut, quads)):

        def local_body(*refs, first=first, last=last):
            local_kernel(*refs, first=first, last=last)

        part, local = call(
            local_body,
            [shape(((last - first) * 2 * rows, 128), F32), shape((rows, sites), F32)],
            [pre_grad, features, near, kernel_one] + ([] if local is None else [local]),
            flops=2 * 256 * sites * 512 * 4 * (last - first),
            name="local",
        )
        halves.append(part)

    def far_body(*refs):
        far_kernel(*refs, sites=sites, held=held)

    sums, far = call(
        far_body,
        [shape((ROWS, 128), BF), shape(((count + 1) * rows, OUTER), BF)],
        [pre_low, pre_mid, pre_high, near_out, feat_out, *halves, two_part],
        flops=2 * 256 * OUTER * OUTER * 48,
        name="far",
    )

    share = ROWS // peers
    parts = lax.all_to_all(sums.reshape(peers, share, 128), AXES, 0, 0, axis_index_groups=plane, tiled=True)

    def plane_sum(parts_ref, out_ref):
        sum_kernel(parts_ref, out_ref, scale=None)

    (partial,) = call(plane_sum, [shape((layers, share, 128), BF)], [parts], name="plane_sum")
    parts = lax.all_to_all(partial, AXES, 0, 0, axis_index_groups=tower, tiled=True)
    scale = float(sites * n_col * n_row) ** (-0.5)

    def tower_sum(parts_ref, out_ref):
        sum_kernel(parts_ref, out_ref, scale=scale)

    (whole,) = call(tower_sum, [shape((peers, share, 128), BF)], [parts], name="tower_sum")
    whole = lax.all_to_all(whole, AXES, 0, 0, axis_index_groups=plane, tiled=True)
    one_grad, two_grad = call(
        unpack_kernel,
        [shape((count, rows, rows), F32), shape((children, rows, wide), F32)],
        [whole.reshape(ROWS, 128)],
        name="unpack",
    )
    (feature_grad,) = call(
        finish_kernel,
        [shape((rows, sites), BF)],
        [local, far, kernel_one, send],
        flops=2 * 256 * OUTER * sites * 4,
        name="finish",
    )
    return feature_grad, one_grad, two_grad.transpose(0, 2, 1)


def solution(mesh):
    placed = (
        P(None, AXES),
        P(None, AXES),
        P(None, AXES),
        P(),
        P(),
        P(None, AXES),
        P(AXES),
        P(AXES),
        P(AXES),
    )
    return jax.shard_map(
        body,
        mesh=mesh,
        in_specs=placed,
        out_specs=(P(None, AXES), P(), P()),
        check_vma=False,
    )
```

```python
import jax
import jax.numpy as jnp
from jax import lax
from jax.experimental import pallas as pl
from jax.experimental.pallas import tpu as pltpu
from jax.sharding import PartitionSpec as P


AXES = ("col", "row")
BF = jnp.bfloat16
F32 = jnp.float32
I32 = jnp.int32
NT = (((1,), (1,)), ((), ()))
NN = (((1,), (0,)), ((), ()))
TN = (((0,), (0,)), ((), ()))
OUTER = 256
ROWS = 1536
XDIM = 4
TILE = 256
AHEAD = 2


def dot(a, b, dims=NN):
    return lax.dot_general(a, b, dims, preferred_element_type=F32)


def onehot(count, width, index, start=0):
    return jnp.where(lax.broadcasted_iota(I32, (count, width), 0) == index - start, 1.0, 0.0).astype(BF)


def call(kernel, outs, args, flops=0, name=None, vmem=16):
    nbytes = sum(a.size * a.dtype.itemsize for a in args) + sum(o.size * o.dtype.itemsize for o in outs)
    return pl.pallas_call(
        kernel,
        out_shape=tuple(outs),
        in_specs=[pl.BlockSpec(memory_space=pltpu.VMEM)] * len(args),
        out_specs=tuple(pl.BlockSpec(memory_space=pltpu.VMEM) for _ in outs),
        cost_estimate=pl.CostEstimate(flops=flops, bytes_accessed=nbytes, transcendentals=0),
        compiler_params=pltpu.CompilerParams(vmem_limit_bytes=vmem << 20),
        name=name,
    )(*args)


def shape(dims, dtype):
    return jax.ShapeDtypeStruct(dims, dtype)


def pack_kernel(grad_ref, out_ref):
    owned = grad_ref.shape[1]
    same = lax.broadcasted_iota(I32, (owned, owned), 0) == lax.broadcasted_iota(I32, (owned, owned), 1)
    out_ref[...] = dot(jnp.where(same, 1.0, 0.0).astype(BF), grad_ref[...], NT).astype(BF)


def outer_kernel(feat_ref, near_ref, send_ref, out_ref, near_out_ref):
    pick = onehot(feat_ref.shape[1], OUTER, send_ref[...])
    out_ref[...] = dot(feat_ref[...], pick).astype(BF)
    near = near_ref[...]
    high = dot((near // 64).astype(BF), pick)
    low = dot((near % 64).astype(BF), pick)
    near_out_ref[...] = (high * 64.0 + low).astype(I32)


def grad_kernel(
    coarse_ref, two_ref, act_in_ref, parent_ref, child_ref, send_ref, pre_ref, pre_out_ref, two_grad_ref
):
    rows, sites = pre_ref.shape
    children = two_ref.shape[0] // rows
    child = child_ref[...]
    parent_grad = dot(coarse_ref[...], onehot(coarse_ref.shape[0], sites, parent_ref[...]), TN).astype(BF)
    stacked = dot(two_ref[...], parent_grad)
    act_grad = stacked[:rows]
    for k in range(1, children):
        act_grad = jnp.where(child == k, stacked[k * rows : (k + 1) * rows], act_grad)
    value = act_in_ref[...].astype(F32)
    gate = 1.0 / (1.0 + jnp.exp(-value))
    pre = (act_grad * gate * (1.0 + value * (1.0 - gate))).astype(BF)
    pre_ref[...] = pre
    pre_out_ref[...] = dot(pre, onehot(sites, OUTER, send_ref[...])).astype(BF)
    act = (value * gate).astype(BF).astype(F32)
    masked = jnp.concatenate([jnp.where(child == k, act, 0.0).astype(BF) for k in range(children)], axis=0)
    two_grad_ref[...] = dot(masked, parent_grad, NT).astype(BF)


def merged(stacked, part, rows):
    blocks = [stacked[k : k + rows] for k in range(0, stacked.shape[0], rows)]
    bit = 1
    while len(blocks) > 1:
        odd = (part & bit) != 0
        blocks = [jnp.where(odd, blocks[k + 1], blocks[k]) for k in range(0, len(blocks), 2)]
        bit *= 2
    return blocks[0].astype(BF)


def gathered(quarters, index, sites, rows):
    place = jnp.where(index < sites, index & (TILE - 1), -1)
    return merged(dot(quarters, onehot(TILE, sites, place)), index // TILE, rows)


def quartered(ref):
    return jnp.concatenate([ref[:, k : k + TILE] for k in range(0, ref.shape[1], TILE)], axis=0)


def ahead_kernel(feat_ref, index_ref, near_ref, *, start):
    rows, sites = feat_ref.shape
    count = index_ref.shape[0]
    quarters = quartered(feat_ref)

    def step(k, carry):
        index = index_ref[pl.ds(jnp.maximum(count - 1 - start - k, 0), 1), :]
        near_ref[pl.ds(pl.multiple_of(k * rows, rows), rows), :] = gathered(quarters, index, sites, rows)
        return carry

    lax.fori_loop(0, near_ref.shape[0] // rows, step, 0, unroll=4)


def local_kernel(pre_ref, feat_ref, index_ref, one_ref, *refs, first, last):
    grads_ref, out_ref = refs[-2:]
    rows, sites = pre_ref.shape
    count = one_ref.shape[0]
    out_ref[...] = refs[0][...] if len(refs) == 3 else jnp.zeros_like(out_ref)
    quarters = quartered(pre_ref)

    def step(g, carry):
        parts, weights = [], []
        for s in range(4):
            q = g * 4 + s
            weights.append(one_ref[jnp.maximum(count - 1 - q, 0)])
            parts.append(gathered(quarters, index_ref[pl.ds(q, 1), :], sites, rows))
        near = jnp.concatenate(parts, axis=0)
        out_ref[...] += dot(jnp.concatenate(weights, axis=0), near, TN)
        grads = dot(feat_ref[...], near, NT)
        for h in range(2):
            start = pl.multiple_of((2 * (g - first) + h) * rows, rows)
            grads_ref[pl.ds(start, rows), :] = grads[:, h * 128 : (h + 1) * 128]
        return carry

    lax.fori_loop(first, last, step, 0)


def late_kernel(pre_ref, index_ref, one_ref, local_ref, out_ref, *, first, last):
    rows, sites = pre_ref.shape
    count = one_ref.shape[0]
    quarters = quartered(pre_ref)
    out_ref[...] = local_ref[...]

    def step(g, carry):
        parts, weights = [], []
        for s in range(4):
            q = g * 4 + s
            weights.append(one_ref[jnp.maximum(count - 1 - q, 0)])
            parts.append(gathered(quarters, index_ref[pl.ds(q, 1), :], sites, rows))
        out_ref[...] += dot(jnp.concatenate(weights, axis=0), jnp.concatenate(parts, axis=0), TN)
        return carry

    lax.fori_loop(first, last, step, 0)


def far_kernel(
    low_ref, mid_ref, high_ref, near_ref, feat_ref, pre_ref, ahead_ref, first_ref, second_ref, two_ref, sums_ref, far_ref, *, sites, held
):
    rows = feat_ref.shape[0]
    refs = (low_ref, mid_ref, high_ref)
    count = near_ref.shape[0]
    split = first_ref.shape[0]
    cut = split + second_ref.shape[0]
    ahead = dot(ahead_ref[...], pre_ref[...], NT)
    group = near_ref[...] - sites
    beside = ((group.astype(F32) + 0.5) * (1.0 / held)).astype(I32)
    place = group - beside * held
    beside = jnp.where(group < 0, -1, beside)
    blocks = []
    for line in range(count // 3):
        dx, dy = line // 3 - 1, line % 3 - 1
        moves = [(mx, my) for mx in sorted({0, dx}) for my in sorted({0, dy}) if (mx, my) != (0, 0)]
        if not moves:
            blocks += [jnp.zeros((rows, OUTER), BF)] * 3
            continue
        tables = jnp.concatenate([refs[my + 1][(mx + 1) * rows : (mx + 2) * rows, :] for mx, my in moves], axis=0)
        lanes = [slice(3 * line + k, 3 * line + k + 1) for k in range(3)]
        index = jnp.concatenate([place[k, :] for k in lanes], axis=1)
        part = jnp.concatenate([beside[k, :] for k in lanes], axis=1)
        stacked = dot(tables, onehot(TILE, 3 * OUTER, index))
        total = jnp.zeros((rows, 3 * OUTER), F32)
        for k, (mx, my) in enumerate(moves):
            total = jnp.where(part == (mx + 1) * 3 + my + 1, stacked[k * rows : (k + 1) * rows], total)
        total = total.astype(BF)
        blocks += [total[:, k * OUTER : (k + 1) * OUTER] for k in range(3)]
    blocks.append(jnp.zeros((rows, OUTER), BF))
    for q, block in enumerate(blocks):
        far_ref[q * rows : (q + 1) * rows, :] = block
    for g in range(len(blocks) // 4):
        both = jnp.concatenate(blocks[4 * g : 4 * g + 4], axis=0)
        grads = dot(feat_ref[...], both, NT)
        for h in range(2):
            start = (2 * g + h) * rows
            if start < split:
                local = first_ref[start : start + rows, :]
            elif start < cut:
                local = second_ref[start - split : start - split + rows, :]
            else:
                k = 2 * (start - cut)
                local = jnp.concatenate([ahead[k : k + rows], ahead[k + rows : k + 2 * rows]], axis=1)
            sums_ref[start : start + rows, :] = (local + grads[:, h * 128 : (h + 1) * 128]).astype(BF)
    base = len(blocks) // 2 * rows
    sums_ref[base : base + two_ref.shape[0], :] = two_ref[...]
    base = base + two_ref.shape[0]
    sums_ref[base:, :] = jnp.zeros((sums_ref.shape[0] - base, 128), BF)


def sum_kernel(parts_ref, out_ref, *, scale):
    total = jnp.sum(parts_ref[...].astype(F32), axis=0)
    if scale is not None:
        total = total * scale
    total = total.astype(out_ref.dtype)
    for k in range(out_ref.shape[0]):
        out_ref[k] = total


def unpack_kernel(sums_ref, one_ref, two_ref):
    count, rows = one_ref.shape[:2]
    for p in range((count + 1) // 2):
        block = sums_ref[p * rows : (p + 1) * rows, :].astype(F32).T
        for h in range(2):
            if 2 * p + h < count:
                one_ref[count - 1 - 2 * p - h] = block[h * rows : (h + 1) * rows, :]
    base = (count + 1) // 2 * rows
    for k in range(two_ref.shape[0]):
        two_ref[k] = sums_ref[base + k * rows : base + (k + 1) * rows, :].astype(F32)


def finish_kernel(local_ref, far_ref, one_ref, send_ref, out_ref):
    rows, sites = local_ref.shape
    count = one_ref.shape[0]
    weights = jnp.concatenate([one_ref[count - 1 - q] for q in range(count)], axis=0)
    total = dot(weights, far_ref[: count * rows, :], TN)
    first = total.astype(BF)
    rest = total - first.astype(F32)
    second = rest.astype(BF)
    third = (rest - second.astype(F32)).astype(BF)
    spread = dot(jnp.concatenate([first, second, third], axis=0), onehot(sites, OUTER, send_ref[...]), NT)
    spread = spread[:rows] + spread[rows : 2 * rows] + spread[2 * rows :]
    out_ref[...] = (local_ref[...] + spread).astype(BF)


def shift(block, axis, step):
    count = lax.axis_size(axis)
    return lax.ppermute(block, axis, [(i, i + step) for i in range(count) if 0 <= i + step < count])


def around(block):
    three = jnp.concatenate([shift(block, "col", 1), block, shift(block, "col", -1)], axis=0)
    return shift(three, "row", 1), three, shift(three, "row", -1)


def body(
    features, preact, coarse_grad, kernel_one, kernel_two, neighbours, send_list, parent_slot, child_pos
):
    rows, sites = features.shape
    count = neighbours.shape[0]
    wide, owned = coarse_grad.shape
    children = kernel_two.shape[0]
    held = send_list.shape[0]
    n_col, n_row = lax.axis_size("col"), lax.axis_size("row")
    peers = XDIM * n_row
    layers = n_col * n_row // peers
    plane = [[z * peers + i for i in range(peers)] for z in range(layers)]
    tower = [[z * peers + i for z in range(layers)] for i in range(peers)]

    (packed,) = call(pack_kernel, [shape((owned, wide), BF)], [coarse_grad], name="pack")
    coarse = lax.all_to_all(packed.reshape(n_col, owned // n_col, wide), "col", 0, 0, tiled=True)
    coarse = coarse.reshape(owned, wide)

    send = jnp.concatenate([send_list, jnp.full((OUTER - held,), -1, I32)])[None, :]
    near = jnp.concatenate([neighbours, jnp.full((1, sites), sites + 9 * held, I32)], axis=0)
    two_rows = kernel_two.transpose(0, 2, 1).reshape(children * rows, wide)
    feat_out, near_out = call(
        outer_kernel,
        [shape((rows, OUTER), BF), shape((count, OUTER), I32)],
        [features, neighbours, send],
        flops=2 * sites * OUTER * 128,
        name="outer",
    )
    pre_grad, pre_out, two_part = call(
        grad_kernel,
        [shape((rows, sites), BF), shape((rows, OUTER), BF), shape((children * rows, wide), BF)],
        [coarse, two_rows, preact, parent_slot[None, :], child_pos[None, :], send],
        flops=2 * 512 * sites * 512,
        name="grads",
    )
    pre_low, pre_mid, pre_high = around(pre_out)

    quads = (count + 3) // 4
    cut = quads - AHEAD
    half = (cut + 1) // 2

    def ahead_body(*refs):
        ahead_kernel(*refs, start=4 * cut)

    (ahead,) = call(
        ahead_body,
        [shape((4 * AHEAD * rows, sites), BF)],
        [features, neighbours],
        flops=2 * 256 * sites * 512 * 4 * AHEAD,
        name="ahead",
    )
    halves, local = [], None
    for first, last in ((0, half), (half, cut)):

        def local_body(*refs, first=first, last=last):
            local_kernel(*refs, first=first, last=last)

        part, local = call(
            local_body,
            [shape(((last - first) * 2 * rows, 128), F32), shape((rows, sites), F32)],
            [pre_grad, features, near, kernel_one] + ([] if local is None else [local]),
            flops=2 * 256 * sites * 512 * 4 * (last - first),
            name="local",
        )
        halves.append(part)

    def far_body(*refs):
        far_kernel(*refs, sites=sites, held=held)

    sums, far = call(
        far_body,
        [shape((ROWS, 128), BF), shape(((count + 1) * rows, OUTER), BF)],
        [pre_low, pre_mid, pre_high, near_out, feat_out, pre_grad, ahead, *halves, two_part],
        flops=2 * 256 * OUTER * OUTER * 48,
        name="far",
    )

    share = ROWS // peers
    parts = lax.all_to_all(sums.reshape(peers, share, 128), AXES, 0, 0, axis_index_groups=plane, tiled=True)

    def plane_sum(parts_ref, out_ref):
        sum_kernel(parts_ref, out_ref, scale=None)

    (partial,) = call(plane_sum, [shape((layers, share, 128), BF)], [parts], name="plane_sum")
    parts = lax.all_to_all(partial, AXES, 0, 0, axis_index_groups=tower, tiled=True)
    scale = float(sites * n_col * n_row) ** (-0.5)

    def tower_sum(parts_ref, out_ref):
        sum_kernel(parts_ref, out_ref, scale=scale)

    (whole,) = call(tower_sum, [shape((peers, share, 128), BF)], [parts], name="tower_sum")
    whole = lax.all_to_all(whole, AXES, 0, 0, axis_index_groups=plane, tiled=True)
    one_grad, two_grad = call(
        unpack_kernel,
        [shape((count, rows, rows), F32), shape((children, rows, wide), F32)],
        [whole.reshape(ROWS, 128)],
        name="unpack",
    )

    def late_body(*refs):
        late_kernel(*refs, first=cut, last=quads)

    (local,) = call(
        late_body,
        [shape((rows, sites), F32)],
        [pre_grad, near, kernel_one, local],
        flops=2 * 256 * sites * 512 * 4 * AHEAD,
        name="late",
    )
    (feature_grad,) = call(
        finish_kernel,
        [shape((rows, sites), BF)],
        [local, far, kernel_one, send],
        flops=2 * 256 * OUTER * sites * 4,
        name="finish",
    )
    return feature_grad, one_grad, two_grad.transpose(0, 2, 1)


def solution(mesh):
    placed = (
        P(None, AXES),
        P(None, AXES),
        P(None, AXES),
        P(),
        P(),
        P(None, AXES),
        P(AXES),
        P(AXES),
        P(AXES),
    )
    return jax.shard_map(
        body,
        mesh=mesh,
        in_specs=placed,
        out_specs=(P(None, AXES), P(), P()),
        check_vma=False,
    )
```

```python
import jax
import jax.numpy as jnp
from jax import lax
from jax.experimental import pallas as pl
from jax.experimental.pallas import tpu as pltpu
from jax.sharding import PartitionSpec as P


AXES = ("col", "row")
BF = jnp.bfloat16
F32 = jnp.float32
I32 = jnp.int32
NT = (((1,), (1,)), ((), ()))
NN = (((1,), (0,)), ((), ()))
TN = (((0,), (0,)), ((), ()))
OUTER = 256
ROWS = 1536
XDIM = 8
TILE = 256
AHEAD = 2


def dot(a, b, dims=NN):
    return lax.dot_general(a, b, dims, preferred_element_type=F32)


def onehot(count, width, index, start=0):
    return jnp.where(lax.broadcasted_iota(I32, (count, width), 0) == index - start, 1.0, 0.0).astype(BF)


def call(kernel, outs, args, flops=0, name=None, vmem=16, scratch=(), scalars=0):
    nbytes = sum(a.size * a.dtype.itemsize for a in args) + sum(o.size * o.dtype.itemsize for o in outs)
    return pl.pallas_call(
        kernel,
        out_shape=tuple(outs),
        in_specs=[pl.BlockSpec(memory_space=pltpu.SMEM)] * scalars
        + [pl.BlockSpec(memory_space=pltpu.VMEM)] * (len(args) - scalars),
        scratch_shapes=list(scratch),
        out_specs=tuple(pl.BlockSpec(memory_space=pltpu.VMEM) for _ in outs),
        cost_estimate=pl.CostEstimate(flops=flops, bytes_accessed=nbytes, transcendentals=0),
        compiler_params=pltpu.CompilerParams(vmem_limit_bytes=vmem << 20),
        name=name,
    )(*args)


def shape(dims, dtype):
    return jax.ShapeDtypeStruct(dims, dtype)


def pack_kernel(grad_ref, out_ref):
    owned = grad_ref.shape[1]
    same = lax.broadcasted_iota(I32, (owned, owned), 0) == lax.broadcasted_iota(I32, (owned, owned), 1)
    out_ref[...] = dot(jnp.where(same, 1.0, 0.0).astype(BF), grad_ref[...], NT).astype(BF)


def outer_kernel(feat_ref, near_ref, send_ref, out_ref, near_out_ref):
    pick = onehot(feat_ref.shape[1], OUTER, send_ref[...])
    out_ref[...] = dot(feat_ref[...], pick).astype(BF)
    near = near_ref[...]
    high = dot((near // 64).astype(BF), pick)
    low = dot((near % 64).astype(BF), pick)
    near_out_ref[...] = (high * 64.0 + low).astype(I32)


def grad_kernel(
    coarse_ref, two_ref, act_in_ref, parent_ref, child_ref, send_ref, pre_ref, pre_out_ref, two_grad_ref
):
    rows, sites = pre_ref.shape
    children = two_ref.shape[0] // rows
    child = child_ref[...]
    parent_grad = dot(coarse_ref[...], onehot(coarse_ref.shape[0], sites, parent_ref[...]), TN).astype(BF)
    stacked = dot(two_ref[...], parent_grad)
    act_grad = stacked[:rows]
    for k in range(1, children):
        act_grad = jnp.where(child == k, stacked[k * rows : (k + 1) * rows], act_grad)
    value = act_in_ref[...].astype(F32)
    gate = 1.0 / (1.0 + jnp.exp(-value))
    pre = (act_grad * gate * (1.0 + value * (1.0 - gate))).astype(BF)
    pre_ref[...] = pre
    pre_out_ref[...] = dot(pre, onehot(sites, OUTER, send_ref[...])).astype(BF)
    act = (value * gate).astype(BF).astype(F32)
    masked = jnp.concatenate([jnp.where(child == k, act, 0.0).astype(BF) for k in range(children)], axis=0)
    two_grad_ref[...] = dot(masked, parent_grad, NT).astype(BF)


def merged(stacked, part, rows):
    blocks = [stacked[k : k + rows] for k in range(0, stacked.shape[0], rows)]
    bit = 1
    while len(blocks) > 1:
        odd = (part & bit) != 0
        blocks = [jnp.where(odd, blocks[k + 1], blocks[k]) for k in range(0, len(blocks), 2)]
        bit *= 2
    return blocks[0].astype(BF)


def gathered(quarters, index, sites, rows):
    place = jnp.where(index < sites, index & (TILE - 1), -1)
    return merged(dot(quarters, onehot(TILE, sites, place)), index // TILE, rows)


def quartered(ref):
    return jnp.concatenate([ref[:, k : k + TILE] for k in range(0, ref.shape[1], TILE)], axis=0)


def ahead_kernel(feat_ref, index_ref, near_ref, *, start):
    rows, sites = feat_ref.shape
    count = index_ref.shape[0]
    quarters = quartered(feat_ref)

    def step(k, carry):
        index = index_ref[pl.ds(jnp.maximum(count - 1 - start - k, 0), 1), :]
        near_ref[pl.ds(pl.multiple_of(k * rows, rows), rows), :] = gathered(quarters, index, sites, rows)
        return carry

    lax.fori_loop(0, near_ref.shape[0] // rows, step, 0, unroll=4)


def local_kernel(pre_ref, feat_ref, index_ref, one_ref, *refs, first, last):
    grads_ref, out_ref = refs[-2:]
    rows, sites = pre_ref.shape
    count = one_ref.shape[0]
    out_ref[...] = refs[0][...] if len(refs) == 3 else jnp.zeros_like(out_ref)
    quarters = quartered(pre_ref)

    def step(g, carry):
        parts, weights = [], []
        for s in range(4):
            q = g * 4 + s
            weights.append(one_ref[jnp.maximum(count - 1 - q, 0)])
            parts.append(gathered(quarters, index_ref[pl.ds(q, 1), :], sites, rows))
        near = jnp.concatenate(parts, axis=0)
        out_ref[...] += dot(jnp.concatenate(weights, axis=0), near, TN)
        grads = dot(feat_ref[...], near, NT)
        for h in range(2):
            start = pl.multiple_of((2 * (g - first) + h) * rows, rows)
            grads_ref[pl.ds(start, rows), :] = grads[:, h * 128 : (h + 1) * 128]
        return carry

    lax.fori_loop(first, last, step, 0)


def late_kernel(pre_ref, index_ref, one_ref, local_ref, out_ref, *, first, last):
    rows, sites = pre_ref.shape
    count = one_ref.shape[0]
    quarters = quartered(pre_ref)
    out_ref[...] = local_ref[...]

    def step(g, carry):
        parts, weights = [], []
        for s in range(4):
            q = g * 4 + s
            weights.append(one_ref[jnp.maximum(count - 1 - q, 0)])
            parts.append(gathered(quarters, index_ref[pl.ds(q, 1), :], sites, rows))
        out_ref[...] += dot(jnp.concatenate(weights, axis=0), jnp.concatenate(parts, axis=0), TN)
        return carry

    lax.fori_loop(first, last, step, 0)


def far_kernel(
    odd_ref, even_ref, mid_ref, other_ref, near_ref, feat_ref, pre_ref, ahead_ref, first_ref, second_ref, two_ref, sums_ref, far_ref, side_ref, *, sites, held
):
    rows = feat_ref.shape[0]
    odd_col, odd_row = odd_ref[0], odd_ref[1]

    @pl.when(odd_row == 0)
    def _():
        side_ref[0] = other_ref[...]
        side_ref[1] = even_ref[...]

    @pl.when(odd_row != 0)
    def _():
        side_ref[0] = even_ref[...]
        side_ref[1] = other_ref[...]

    refs = (side_ref.at[0], mid_ref, side_ref.at[1])
    low = pl.multiple_of((1 - odd_col) * 2 * rows, rows)
    columns = (low, rows, pl.multiple_of(2 * rows - low, rows))
    count = near_ref.shape[0]
    split = first_ref.shape[0]
    cut = split + second_ref.shape[0]
    ahead = dot(ahead_ref[...], pre_ref[...], NT)
    group = near_ref[...] - sites
    beside = ((group.astype(F32) + 0.5) * (1.0 / held)).astype(I32)
    place = group - beside * held
    beside = jnp.where(group < 0, -1, beside)
    blocks = []
    for line in range(count // 3):
        dx, dy = line // 3 - 1, line % 3 - 1
        moves = [(mx, my) for mx in sorted({0, dx}) for my in sorted({0, dy}) if (mx, my) != (0, 0)]
        if not moves:
            blocks += [jnp.zeros((rows, OUTER), BF)] * 3
            continue
        tables = jnp.concatenate([refs[my + 1][pl.ds(columns[mx + 1], rows), :] for mx, my in moves], axis=0)
        lanes = [slice(3 * line + k, 3 * line + k + 1) for k in range(3)]
        index = jnp.concatenate([place[k, :] for k in lanes], axis=1)
        part = jnp.concatenate([beside[k, :] for k in lanes], axis=1)
        stacked = dot(tables, onehot(TILE, 3 * OUTER, index))
        total = jnp.zeros((rows, 3 * OUTER), F32)
        for k, (mx, my) in enumerate(moves):
            total = jnp.where(part == (mx + 1) * 3 + my + 1, stacked[k * rows : (k + 1) * rows], total)
        total = total.astype(BF)
        blocks += [total[:, k * OUTER : (k + 1) * OUTER] for k in range(3)]
    blocks.append(jnp.zeros((rows, OUTER), BF))
    for q, block in enumerate(blocks):
        far_ref[q * rows : (q + 1) * rows, :] = block
    for g in range(len(blocks) // 4):
        both = jnp.concatenate(blocks[4 * g : 4 * g + 4], axis=0)
        grads = dot(feat_ref[...], both, NT)
        for h in range(2):
            start = (2 * g + h) * rows
            if start < split:
                local = first_ref[start : start + rows, :]
            elif start < cut:
                local = second_ref[start - split : start - split + rows, :]
            else:
                k = 2 * (start - cut)
                local = jnp.concatenate([ahead[k : k + rows], ahead[k + rows : k + 2 * rows]], axis=1)
            sums_ref[start : start + rows, :] = (local + grads[:, h * 128 : (h + 1) * 128]).astype(BF)
    base = len(blocks) // 2 * rows
    sums_ref[base : base + two_ref.shape[0], :] = two_ref[...]
    base = base + two_ref.shape[0]
    sums_ref[base:, :] = jnp.zeros((sums_ref.shape[0] - base, 128), BF)


def sum_kernel(parts_ref, out_ref, *, scale):
    total = jnp.sum(parts_ref[...].astype(F32), axis=0)
    if scale is not None:
        total = total * scale
    total = total.astype(out_ref.dtype)
    for k in range(out_ref.shape[0]):
        out_ref[k] = total


def unpack_kernel(sums_ref, one_ref, two_ref):
    count, rows = one_ref.shape[:2]
    for p in range((count + 1) // 2):
        block = sums_ref[p * rows : (p + 1) * rows, :].astype(F32).T
        for h in range(2):
            if 2 * p + h < count:
                one_ref[count - 1 - 2 * p - h] = block[h * rows : (h + 1) * rows, :]
    base = (count + 1) // 2 * rows
    for k in range(two_ref.shape[0]):
        two_ref[k] = sums_ref[base + k * rows : base + (k + 1) * rows, :].astype(F32)


def finish_kernel(local_ref, far_ref, one_ref, send_ref, out_ref):
    rows, sites = local_ref.shape
    count = one_ref.shape[0]
    weights = jnp.concatenate([one_ref[count - 1 - q] for q in range(count)], axis=0)
    total = dot(weights, far_ref[: count * rows, :], TN)
    first = total.astype(BF)
    rest = total - first.astype(F32)
    second = rest.astype(BF)
    third = (rest - second.astype(F32)).astype(BF)
    spread = dot(jnp.concatenate([first, second, third], axis=0), onehot(sites, OUTER, send_ref[...]), NT)
    spread = spread[:rows] + spread[rows : 2 * rows] + spread[2 * rows :]
    out_ref[...] = (local_ref[...] + spread).astype(BF)


def swap(block, axis, first):
    count = lax.axis_size(axis)
    pairs = [(i, i + 1) for i in range(first, count - 1, 2)]
    return lax.ppermute(block, axis, pairs + [(j, i) for i, j in pairs])


def around(block):
    three = jnp.concatenate([swap(block, "col", 0), block, swap(block, "col", 1)], axis=0)
    return swap(three, "row", 0), three, swap(three, "row", 1)


def body(
    features, preact, coarse_grad, kernel_one, kernel_two, neighbours, send_list, parent_slot, child_pos
):
    rows, sites = features.shape
    count = neighbours.shape[0]
    wide, owned = coarse_grad.shape
    children = kernel_two.shape[0]
    held = send_list.shape[0]
    n_col, n_row = lax.axis_size("col"), lax.axis_size("row")
    peers = XDIM * n_row
    layers = n_col * n_row // peers
    plane = [[z * peers + i for i in range(peers)] for z in range(layers)]
    tower = [[z * peers + i for z in range(layers)] for i in range(peers)]

    (packed,) = call(pack_kernel, [shape((owned, wide), BF)], [coarse_grad], name="pack")
    coarse = lax.all_to_all(packed.reshape(n_col, owned // n_col, wide), "col", 0, 0, tiled=True)
    coarse = coarse.reshape(owned, wide)

    odd = jnp.stack([lax.axis_index("col") % 2, lax.axis_index("row") % 2])
    send = jnp.concatenate([send_list, jnp.full((OUTER - held,), -1, I32)])[None, :]
    near = jnp.concatenate([neighbours, jnp.full((1, sites), sites + 9 * held, I32)], axis=0)
    two_rows = kernel_two.transpose(0, 2, 1).reshape(children * rows, wide)
    feat_out, near_out = call(
        outer_kernel,
        [shape((rows, OUTER), BF), shape((count, OUTER), I32)],
        [features, neighbours, send],
        flops=2 * sites * OUTER * 128,
        name="outer",
    )
    pre_grad, pre_out, two_part = call(
        grad_kernel,
        [shape((rows, sites), BF), shape((rows, OUTER), BF), shape((children * rows, wide), BF)],
        [coarse, two_rows, preact, parent_slot[None, :], child_pos[None, :], send],
        flops=2 * 512 * sites * 512,
        name="grads",
    )
    pre_low, pre_mid, pre_high = around(pre_out)

    quads = (count + 3) // 4
    cut = quads - AHEAD
    half = (cut + 1) // 2

    def ahead_body(*refs):
        ahead_kernel(*refs, start=4 * cut)

    (ahead,) = call(
        ahead_body,
        [shape((4 * AHEAD * rows, sites), BF)],
        [features, neighbours],
        flops=2 * 256 * sites * 512 * 4 * AHEAD,
        name="ahead",
    )
    halves, local = [], None
    for first, last in ((0, half), (half, cut)):

        def local_body(*refs, first=first, last=last):
            local_kernel(*refs, first=first, last=last)

        part, local = call(
            local_body,
            [shape(((last - first) * 2 * rows, 128), F32), shape((rows, sites), F32)],
            [pre_grad, features, near, kernel_one] + ([] if local is None else [local]),
            flops=2 * 256 * sites * 512 * 4 * (last - first),
            name="local",
        )
        halves.append(part)

    def far_body(*refs):
        far_kernel(*refs, sites=sites, held=held)

    sums, far = call(
        far_body,
        [shape((ROWS, 128), BF), shape(((count + 1) * rows, OUTER), BF)],
        [odd, pre_low, pre_mid, pre_high, near_out, feat_out, pre_grad, ahead, *halves, two_part],
        flops=2 * 256 * OUTER * OUTER * 48,
        scratch=[pltpu.VMEM((2, 3 * rows, OUTER), BF)],
        scalars=1,
        name="far",
    )

    share = ROWS // peers
    parts = lax.all_to_all(sums.reshape(peers, share, 128), AXES, 0, 0, axis_index_groups=plane, tiled=True)

    def plane_sum(parts_ref, out_ref):
        sum_kernel(parts_ref, out_ref, scale=None)

    (partial,) = call(plane_sum, [shape((layers, share, 128), BF)], [parts], name="plane_sum")
    parts = lax.all_to_all(partial, AXES, 0, 0, axis_index_groups=tower, tiled=True)
    scale = float(sites * n_col * n_row) ** (-0.5)

    def tower_sum(parts_ref, out_ref):
        sum_kernel(parts_ref, out_ref, scale=scale)

    (whole,) = call(tower_sum, [shape((peers, share, 128), BF)], [parts], name="tower_sum")
    whole = lax.all_to_all(whole, AXES, 0, 0, axis_index_groups=plane, tiled=True)
    one_grad, two_grad = call(
        unpack_kernel,
        [shape((count, rows, rows), F32), shape((children, rows, wide), F32)],
        [whole.reshape(ROWS, 128)],
        name="unpack",
    )

    def late_body(*refs):
        late_kernel(*refs, first=cut, last=quads)

    (local,) = call(
        late_body,
        [shape((rows, sites), F32)],
        [pre_grad, near, kernel_one, local],
        flops=2 * 256 * sites * 512 * 4 * AHEAD,
        name="late",
    )
    (feature_grad,) = call(
        finish_kernel,
        [shape((rows, sites), BF)],
        [local, far, kernel_one, send],
        flops=2 * 256 * OUTER * sites * 4,
        name="finish",
    )
    return feature_grad, one_grad, two_grad.transpose(0, 2, 1)


def solution(mesh):
    placed = (
        P(None, AXES),
        P(None, AXES),
        P(None, AXES),
        P(),
        P(),
        P(None, AXES),
        P(AXES),
        P(AXES),
        P(AXES),
    )
    return jax.shard_map(
        body,
        mesh=mesh,
        in_specs=placed,
        out_specs=(P(None, AXES), P(), P()),
        check_vma=False,
    )
```

```python
import jax
import jax.numpy as jnp
from jax import lax
from jax.experimental import pallas as pl
from jax.experimental.pallas import tpu as pltpu
from jax.sharding import PartitionSpec as P


AXES = ("col", "row")
BF = jnp.bfloat16
F32 = jnp.float32
I32 = jnp.int32
NT = (((1,), (1,)), ((), ()))
NN = (((1,), (0,)), ((), ()))
TN = (((0,), (0,)), ((), ()))
OUTER = 256
ROWS = 1536
XDIM = 8
TILE = 256
AHEAD = 2


def dot(a, b, dims=NN):
    return lax.dot_general(a, b, dims, preferred_element_type=F32)


def onehot(count, width, index, start=0):
    return jnp.where(lax.broadcasted_iota(I32, (count, width), 0) == index - start, 1.0, 0.0).astype(BF)


def call(kernel, outs, args, flops=0, name=None, vmem=16, scratch=(), scalars=0):
    nbytes = sum(a.size * a.dtype.itemsize for a in args) + sum(o.size * o.dtype.itemsize for o in outs)
    return pl.pallas_call(
        kernel,
        out_shape=tuple(outs),
        in_specs=[pl.BlockSpec(memory_space=pltpu.SMEM)] * scalars
        + [pl.BlockSpec(memory_space=pltpu.VMEM)] * (len(args) - scalars),
        scratch_shapes=list(scratch),
        out_specs=tuple(pl.BlockSpec(memory_space=pltpu.VMEM) for _ in outs),
        cost_estimate=pl.CostEstimate(flops=flops, bytes_accessed=nbytes, transcendentals=0),
        compiler_params=pltpu.CompilerParams(vmem_limit_bytes=vmem << 20),
        name=name,
    )(*args)


def shape(dims, dtype):
    return jax.ShapeDtypeStruct(dims, dtype)


def pack_kernel(grad_ref, out_ref):
    owned = grad_ref.shape[1]
    same = lax.broadcasted_iota(I32, (owned, owned), 0) == lax.broadcasted_iota(I32, (owned, owned), 1)
    out_ref[...] = dot(jnp.where(same, 1.0, 0.0).astype(BF), grad_ref[...], NT).astype(BF)


def grad_kernel(
    coarse_ref, two_ref, act_in_ref, parent_ref, child_ref, send_ref, pre_ref, pre_out_ref, two_grad_ref
):
    rows, sites = pre_ref.shape
    children = two_ref.shape[0] // rows
    child = child_ref[...]
    parent_grad = dot(coarse_ref[...], onehot(coarse_ref.shape[0], sites, parent_ref[...]), TN).astype(BF)
    stacked = dot(two_ref[...], parent_grad)
    act_grad = stacked[:rows]
    for k in range(1, children):
        act_grad = jnp.where(child == k, stacked[k * rows : (k + 1) * rows], act_grad)
    value = act_in_ref[...].astype(F32)
    gate = 1.0 / (1.0 + jnp.exp(-value))
    pre = (act_grad * gate * (1.0 + value * (1.0 - gate))).astype(BF)
    pre_ref[...] = pre
    pre_out_ref[...] = dot(pre, onehot(sites, OUTER, send_ref[...])).astype(BF)
    act = (value * gate).astype(BF).astype(F32)
    masked = jnp.concatenate([jnp.where(child == k, act, 0.0).astype(BF) for k in range(children)], axis=0)
    two_grad_ref[...] = dot(masked, parent_grad, NT).astype(BF)


def merged(stacked, part, rows):
    blocks = [stacked[k : k + rows] for k in range(0, stacked.shape[0], rows)]
    bit = 1
    while len(blocks) > 1:
        odd = (part & bit) != 0
        blocks = [jnp.where(odd, blocks[k + 1], blocks[k]) for k in range(0, len(blocks), 2)]
        bit *= 2
    return blocks[0].astype(BF)


def gathered(quarters, index, sites, rows):
    place = jnp.where(index < sites, index & (TILE - 1), -1)
    return merged(dot(quarters, onehot(TILE, sites, place)), index // TILE, rows)


def quartered(ref):
    return jnp.concatenate([ref[:, k : k + TILE] for k in range(0, ref.shape[1], TILE)], axis=0)


def ahead_kernel(feat_ref, index_ref, send_ref, near_ref, out_ref, index_out_ref, *, start):
    rows, sites = feat_ref.shape
    count = index_ref.shape[0]
    pick = onehot(sites, OUTER, send_ref[...])
    out_ref[...] = dot(feat_ref[...], pick).astype(BF)
    index = index_ref[...]
    high = dot((index // 64).astype(BF), pick)
    low = dot((index % 64).astype(BF), pick)
    index_out_ref[...] = (high * 64.0 + low).astype(I32)
    quarters = quartered(feat_ref)

    def step(k, carry):
        index = index_ref[pl.ds(jnp.maximum(count - 1 - start - k, 0), 1), :]
        near_ref[pl.ds(pl.multiple_of(k * rows, rows), rows), :] = gathered(quarters, index, sites, rows)
        return carry

    lax.fori_loop(0, near_ref.shape[0] // rows, step, 0, unroll=4)


def local_kernel(pre_ref, feat_ref, index_ref, one_ref, *refs, first, last):
    grads_ref, out_ref = refs[-2:]
    rows, sites = pre_ref.shape
    count = one_ref.shape[0]
    out_ref[...] = refs[0][...] if len(refs) == 3 else jnp.zeros_like(out_ref)
    quarters = quartered(pre_ref)

    def step(g, carry):
        parts, weights = [], []
        for s in range(4):
            q = g * 4 + s
            weights.append(one_ref[jnp.maximum(count - 1 - q, 0)])
            parts.append(gathered(quarters, index_ref[pl.ds(q, 1), :], sites, rows))
        near = jnp.concatenate(parts, axis=0)
        out_ref[...] += dot(jnp.concatenate(weights, axis=0), near, TN)
        grads = dot(feat_ref[...], near, NT)
        for h in range(2):
            start = pl.multiple_of((2 * (g - first) + h) * rows, rows)
            grads_ref[pl.ds(start, rows), :] = grads[:, h * 128 : (h + 1) * 128]
        return carry

    lax.fori_loop(first, last, step, 0)


def late_kernel(pre_ref, index_ref, one_ref, local_ref, out_ref, *, first, last):
    rows, sites = pre_ref.shape
    count = one_ref.shape[0]
    quarters = quartered(pre_ref)
    out_ref[...] = local_ref[...]

    def step(g, carry):
        parts, weights = [], []
        for s in range(4):
            q = g * 4 + s
            weights.append(one_ref[jnp.maximum(count - 1 - q, 0)])
            parts.append(gathered(quarters, index_ref[pl.ds(q, 1), :], sites, rows))
        out_ref[...] += dot(jnp.concatenate(weights, axis=0), jnp.concatenate(parts, axis=0), TN)
        return carry

    lax.fori_loop(first, last, step, 0)


def far_kernel(
    odd_ref, even_ref, mid_ref, other_ref, near_ref, feat_ref, pre_ref, ahead_ref, first_ref, second_ref, two_ref, sums_ref, far_ref, *, sites, held
):
    rows = feat_ref.shape[0]
    odd_col, odd_row = odd_ref[0] != 0, odd_ref[1] != 0

    def side(flag, low, high):
        return jnp.where(flag, high, low), jnp.where(flag, low, high)

    tables = {}
    lines = (*side(odd_row, other_ref[...], even_ref[...]), mid_ref[...])
    for my, line in zip((-1, 1, 0), lines):
        last, following = side(odd_col, line[2 * rows :], line[:rows])
        tables[-1, my], tables[0, my], tables[1, my] = last, line[rows : 2 * rows], following
    count = near_ref.shape[0]
    split = first_ref.shape[0]
    cut = split + second_ref.shape[0]
    ahead = dot(ahead_ref[...], pre_ref[...], NT)
    group = near_ref[...] - sites
    beside = ((group.astype(F32) + 0.5) * (1.0 / held)).astype(I32)
    place = group - beside * held
    beside = jnp.where(group < 0, -1, beside)
    blocks = []
    for line in range(count // 3):
        dx, dy = line // 3 - 1, line % 3 - 1
        moves = [(mx, my) for mx in sorted({0, dx}) for my in sorted({0, dy}) if (mx, my) != (0, 0)]
        if not moves:
            blocks += [jnp.zeros((rows, OUTER), BF)] * 3
            continue
        choice = jnp.concatenate([tables[move] for move in moves], axis=0)
        lanes = [slice(3 * line + k, 3 * line + k + 1) for k in range(3)]
        index = jnp.concatenate([place[k, :] for k in lanes], axis=1)
        part = jnp.concatenate([beside[k, :] for k in lanes], axis=1)
        stacked = dot(choice, onehot(TILE, 3 * OUTER, index))
        total = jnp.zeros((rows, 3 * OUTER), F32)
        for k, (mx, my) in enumerate(moves):
            total = jnp.where(part == (mx + 1) * 3 + my + 1, stacked[k * rows : (k + 1) * rows], total)
        total = total.astype(BF)
        blocks += [total[:, k * OUTER : (k + 1) * OUTER] for k in range(3)]
    blocks.append(jnp.zeros((rows, OUTER), BF))
    for q, block in enumerate(blocks):
        far_ref[q * rows : (q + 1) * rows, :] = block
    for g in range(len(blocks) // 4):
        both = jnp.concatenate(blocks[4 * g : 4 * g + 4], axis=0)
        grads = dot(feat_ref[...], both, NT)
        for h in range(2):
            start = (2 * g + h) * rows
            if start < split:
                local = first_ref[start : start + rows, :]
            elif start < cut:
                local = second_ref[start - split : start - split + rows, :]
            else:
                k = 2 * (start - cut)
                local = jnp.concatenate([ahead[k : k + rows], ahead[k + rows : k + 2 * rows]], axis=1)
            sums_ref[start : start + rows, :] = (local + grads[:, h * 128 : (h + 1) * 128]).astype(BF)
    base = len(blocks) // 2 * rows
    sums_ref[base : base + two_ref.shape[0], :] = two_ref[...]
    base = base + two_ref.shape[0]
    sums_ref[base:, :] = jnp.zeros((sums_ref.shape[0] - base, 128), BF)


def sum_kernel(parts_ref, out_ref, *, scale):
    total = jnp.sum(parts_ref[...].astype(F32), axis=0)
    if scale is not None:
        total = total * scale
    total = total.astype(out_ref.dtype)
    for k in range(out_ref.shape[0]):
        out_ref[k] = total


def unpack_kernel(sums_ref, one_ref, two_ref):
    count, rows = one_ref.shape[:2]
    for p in range((count + 1) // 2):
        block = sums_ref[p * rows : (p + 1) * rows, :].astype(F32).T
        for h in range(2):
            if 2 * p + h < count:
                one_ref[count - 1 - 2 * p - h] = block[h * rows : (h + 1) * rows, :]
    base = (count + 1) // 2 * rows
    for k in range(two_ref.shape[0]):
        two_ref[k] = sums_ref[base + k * rows : base + (k + 1) * rows, :].astype(F32)


def finish_kernel(local_ref, far_ref, one_ref, send_ref, out_ref):
    rows, sites = local_ref.shape
    count = one_ref.shape[0]
    weights = jnp.concatenate([one_ref[count - 1 - q] for q in range(count)], axis=0)
    total = dot(weights, far_ref[: count * rows, :], TN)
    first = total.astype(BF)
    rest = total - first.astype(F32)
    second = rest.astype(BF)
    third = (rest - second.astype(F32)).astype(BF)
    spread = dot(jnp.concatenate([first, second, third], axis=0), onehot(sites, OUTER, send_ref[...]), NT)
    spread = spread[:rows] + spread[rows : 2 * rows] + spread[2 * rows :]
    out_ref[...] = (local_ref[...] + spread).astype(BF)


def swap(block, axis, first):
    count = lax.axis_size(axis)
    pairs = [(i, i + 1) for i in range(first, count - 1, 2)]
    return lax.ppermute(block, axis, pairs + [(j, i) for i, j in pairs])


def around(block):
    three = jnp.concatenate([swap(block, "col", 0), block, swap(block, "col", 1)], axis=0)
    return swap(three, "row", 0), three, swap(three, "row", 1)


def body(
    features, preact, coarse_grad, kernel_one, kernel_two, neighbours, send_list, parent_slot, child_pos
):
    rows, sites = features.shape
    count = neighbours.shape[0]
    wide, owned = coarse_grad.shape
    children = kernel_two.shape[0]
    held = send_list.shape[0]
    n_col, n_row = lax.axis_size("col"), lax.axis_size("row")
    peers = XDIM * n_row
    layers = n_col * n_row // peers
    plane = [[z * peers + i for i in range(peers)] for z in range(layers)]
    tower = [[z * peers + i for z in range(layers)] for i in range(peers)]

    (packed,) = call(pack_kernel, [shape((owned, wide), BF)], [coarse_grad], name="pack")
    coarse = lax.all_to_all(packed.reshape(n_col, owned // n_col, wide), "col", 0, 0, tiled=True)
    coarse = coarse.reshape(owned, wide)

    odd = jnp.stack([lax.axis_index("col") % 2, lax.axis_index("row") % 2])
    send = jnp.concatenate([send_list, jnp.full((OUTER - held,), -1, I32)])[None, :]
    near = jnp.concatenate([neighbours, jnp.full((1, sites), sites + 9 * held, I32)], axis=0)
    two_rows = kernel_two.transpose(0, 2, 1).reshape(children * rows, wide)
    pre_grad, pre_out, two_part = call(
        grad_kernel,
        [shape((rows, sites), BF), shape((rows, OUTER), BF), shape((children * rows, wide), BF)],
        [coarse, two_rows, preact, parent_slot[None, :], child_pos[None, :], send],
        flops=2 * 512 * sites * 512,
        name="grads",
    )
    pre_low, pre_mid, pre_high = around(pre_out)

    quads = (count + 3) // 4
    cut = quads - AHEAD
    half = (cut + 1) // 2

    def ahead_body(*refs):
        ahead_kernel(*refs, start=4 * cut)

    ahead, feat_out, near_out = call(
        ahead_body,
        [shape((4 * AHEAD * rows, sites), BF), shape((rows, OUTER), BF), shape((count, OUTER), I32)],
        [features, neighbours, send],
        flops=2 * 256 * sites * 512 * 4 * AHEAD,
        name="ahead",
    )
    halves, local = [], None
    for first, last in ((0, half), (half, cut)):

        def local_body(*refs, first=first, last=last):
            local_kernel(*refs, first=first, last=last)

        part, local = call(
            local_body,
            [shape(((last - first) * 2 * rows, 128), F32), shape((rows, sites), F32)],
            [pre_grad, features, near, kernel_one] + ([] if local is None else [local]),
            flops=2 * 256 * sites * 512 * 4 * (last - first),
            name="local",
        )
        halves.append(part)

    def far_body(*refs):
        far_kernel(*refs, sites=sites, held=held)

    sums, far = call(
        far_body,
        [shape((ROWS, 128), BF), shape(((count + 1) * rows, OUTER), BF)],
        [odd, pre_low, pre_mid, pre_high, near_out, feat_out, pre_grad, ahead, *halves, two_part],
        flops=2 * 256 * OUTER * OUTER * 48,
        scalars=1,
        name="far",
    )

    share = ROWS // peers
    parts = lax.all_to_all(sums.reshape(peers, share, 128), AXES, 0, 0, axis_index_groups=plane, tiled=True)

    def plane_sum(parts_ref, out_ref):
        sum_kernel(parts_ref, out_ref, scale=None)

    (partial,) = call(plane_sum, [shape((layers, share, 128), BF)], [parts], name="plane_sum")
    parts = lax.all_to_all(partial, AXES, 0, 0, axis_index_groups=tower, tiled=True)
    scale = float(sites * n_col * n_row) ** (-0.5)

    def tower_sum(parts_ref, out_ref):
        sum_kernel(parts_ref, out_ref, scale=scale)

    (whole,) = call(tower_sum, [shape((peers, share, 128), BF)], [parts], name="tower_sum")
    whole = lax.all_to_all(whole, AXES, 0, 0, axis_index_groups=plane, tiled=True)
    one_grad, two_grad = call(
        unpack_kernel,
        [shape((count, rows, rows), F32), shape((children, rows, wide), F32)],
        [whole.reshape(ROWS, 128)],
        name="unpack",
    )

    def late_body(*refs):
        late_kernel(*refs, first=cut, last=quads)

    (local,) = call(
        late_body,
        [shape((rows, sites), F32)],
        [pre_grad, near, kernel_one, local],
        flops=2 * 256 * sites * 512 * 4 * AHEAD,
        name="late",
    )
    (feature_grad,) = call(
        finish_kernel,
        [shape((rows, sites), BF)],
        [local, far, kernel_one, send],
        flops=2 * 256 * OUTER * sites * 4,
        name="finish",
    )
    return feature_grad, one_grad, two_grad.transpose(0, 2, 1)


def solution(mesh):
    placed = (
        P(None, AXES),
        P(None, AXES),
        P(None, AXES),
        P(),
        P(),
        P(None, AXES),
        P(AXES),
        P(AXES),
        P(AXES),
    )
    return jax.shard_map(
        body,
        mesh=mesh,
        in_specs=placed,
        out_specs=(P(None, AXES), P(), P()),
        check_vma=False,
    )
```

```python
import jax
import jax.numpy as jnp
from jax import lax
from jax.experimental import pallas as pl
from jax.experimental.pallas import tpu as pltpu
from jax.sharding import PartitionSpec as P


AXES = ("col", "row")
BF = jnp.bfloat16
F32 = jnp.float32
I32 = jnp.int32
NT = (((1,), (1,)), ((), ()))
NN = (((1,), (0,)), ((), ()))
TN = (((0,), (0,)), ((), ()))
OUTER = 256
ROWS = 1536
XDIM = 8
TILE = 256
AHEAD = 2


def dot(a, b, dims=NN):
    return lax.dot_general(a, b, dims, preferred_element_type=F32)


def onehot(count, width, index, start=0):
    return jnp.where(lax.broadcasted_iota(I32, (count, width), 0) == index - start, 1.0, 0.0).astype(BF)


def call(kernel, outs, args, flops=0, name=None, vmem=16, scratch=(), scalars=0):
    nbytes = sum(a.size * a.dtype.itemsize for a in args) + sum(o.size * o.dtype.itemsize for o in outs)
    return pl.pallas_call(
        kernel,
        out_shape=tuple(outs),
        in_specs=[pl.BlockSpec(memory_space=pltpu.SMEM)] * scalars
        + [pl.BlockSpec(memory_space=pltpu.VMEM)] * (len(args) - scalars),
        scratch_shapes=list(scratch),
        out_specs=tuple(pl.BlockSpec(memory_space=pltpu.VMEM) for _ in outs),
        cost_estimate=pl.CostEstimate(flops=flops, bytes_accessed=nbytes, transcendentals=0),
        compiler_params=pltpu.CompilerParams(vmem_limit_bytes=vmem << 20),
        name=name,
    )(*args)


def shape(dims, dtype):
    return jax.ShapeDtypeStruct(dims, dtype)


def pack_kernel(grad_ref, out_ref):
    owned = grad_ref.shape[1]
    same = lax.broadcasted_iota(I32, (owned, owned), 0) == lax.broadcasted_iota(I32, (owned, owned), 1)
    out_ref[...] = dot(jnp.where(same, 1.0, 0.0).astype(BF), grad_ref[...], NT).astype(BF)


def grad_kernel(
    coarse_ref, two_ref, act_in_ref, parent_ref, child_ref, send_ref, pre_ref, pre_out_ref, two_grad_ref
):
    rows, sites = pre_ref.shape
    children = two_ref.shape[0] // rows
    child = child_ref[...]
    parent_grad = dot(coarse_ref[...], onehot(coarse_ref.shape[0], sites, parent_ref[...]), TN).astype(BF)
    stacked = dot(two_ref[...], parent_grad)
    act_grad = stacked[:rows]
    for k in range(1, children):
        act_grad = jnp.where(child == k, stacked[k * rows : (k + 1) * rows], act_grad)
    value = act_in_ref[...].astype(F32)
    gate = 1.0 / (1.0 + jnp.exp(-value))
    pre = (act_grad * gate * (1.0 + value * (1.0 - gate))).astype(BF)
    pre_ref[...] = pre
    pre_out_ref[...] = dot(pre, onehot(sites, OUTER, send_ref[...])).astype(BF)
    act = (value * gate).astype(BF).astype(F32)
    masked = jnp.concatenate([jnp.where(child == k, act, 0.0).astype(BF) for k in range(children)], axis=0)
    two_grad_ref[...] = dot(masked, parent_grad, NT).astype(BF)


def merged(stacked, part, rows):
    blocks = [stacked[k : k + rows] for k in range(0, stacked.shape[0], rows)]
    bit = 1
    while len(blocks) > 1:
        odd = (part & bit) != 0
        blocks = [jnp.where(odd, blocks[k + 1], blocks[k]) for k in range(0, len(blocks), 2)]
        bit *= 2
    return blocks[0].astype(BF)


def gathered(quarters, index, sites, rows):
    place = jnp.where(index < sites, index & (TILE - 1), -1)
    return merged(dot(quarters, onehot(TILE, sites, place)), index // TILE, rows)


def quartered(ref):
    return jnp.concatenate([ref[:, k : k + TILE] for k in range(0, ref.shape[1], TILE)], axis=0)


def ahead_kernel(feat_ref, index_ref, send_ref, near_ref, out_ref, index_out_ref, *, start):
    rows, sites = feat_ref.shape
    count = index_ref.shape[0]
    pick = onehot(sites, OUTER, send_ref[...])
    out_ref[...] = dot(feat_ref[...], pick).astype(BF)
    index = index_ref[...]
    high = dot((index // 64).astype(BF), pick)
    low = dot((index % 64).astype(BF), pick)
    index_out_ref[...] = (high * 64.0 + low).astype(I32)
    quarters = quartered(feat_ref)

    def step(k, carry):
        index = index_ref[pl.ds(jnp.maximum(count - 1 - start - k, 0), 1), :]
        near_ref[pl.ds(pl.multiple_of(k * rows, rows), rows), :] = gathered(quarters, index, sites, rows)
        return carry

    lax.fori_loop(0, near_ref.shape[0] // rows, step, 0, unroll=4)


def local_kernel(pre_ref, feat_ref, index_ref, one_ref, *refs, first, last):
    grads_ref, out_ref = refs[-2:]
    rows, sites = pre_ref.shape
    count = one_ref.shape[0]
    out_ref[...] = refs[0][...] if len(refs) == 3 else jnp.zeros_like(out_ref)
    quarters = quartered(pre_ref)

    def step(g, carry):
        parts, weights = [], []
        for s in range(4):
            q = g * 4 + s
            weights.append(one_ref[jnp.maximum(count - 1 - q, 0)])
            parts.append(gathered(quarters, index_ref[pl.ds(q, 1), :], sites, rows))
        near = jnp.concatenate(parts, axis=0)
        out_ref[...] += dot(jnp.concatenate(weights, axis=0), near, TN)
        grads = dot(feat_ref[...], near, NT)
        for h in range(2):
            start = pl.multiple_of((2 * (g - first) + h) * rows, rows)
            grads_ref[pl.ds(start, rows), :] = grads[:, h * 128 : (h + 1) * 128]
        return carry

    lax.fori_loop(first, last, step, 0)


def late_kernel(pre_ref, index_ref, one_ref, local_ref, out_ref, *, first, last):
    rows, sites = pre_ref.shape
    count = one_ref.shape[0]
    quarters = quartered(pre_ref)
    out_ref[...] = local_ref[...]

    def step(g, carry):
        parts, weights = [], []
        for s in range(4):
            q = g * 4 + s
            weights.append(one_ref[jnp.maximum(count - 1 - q, 0)])
            parts.append(gathered(quarters, index_ref[pl.ds(q, 1), :], sites, rows))
        out_ref[...] += dot(jnp.concatenate(weights, axis=0), jnp.concatenate(parts, axis=0), TN)
        return carry

    lax.fori_loop(first, last, step, 0)


def far_kernel(
    low_ref, mid_ref, high_ref, near_ref, feat_ref, pre_ref, ahead_ref, first_ref, second_ref, two_ref, sums_ref, far_ref, *, sites, held
):
    rows = feat_ref.shape[0]
    tables = {}
    for my, line in ((-1, low_ref), (0, mid_ref), (1, high_ref)):
        for mx in (-1, 0, 1):
            tables[mx, my] = line[(mx + 1) * rows : (mx + 2) * rows, :]
    count = near_ref.shape[0]
    split = first_ref.shape[0]
    cut = split + second_ref.shape[0]
    ahead = dot(ahead_ref[...], pre_ref[...], NT)
    group = near_ref[...] - sites
    beside = ((group.astype(F32) + 0.5) * (1.0 / held)).astype(I32)
    place = group - beside * held
    beside = jnp.where(group < 0, -1, beside)
    blocks = []
    for line in range(count // 3):
        dx, dy = line // 3 - 1, line % 3 - 1
        moves = [(mx, my) for mx in sorted({0, dx}) for my in sorted({0, dy}) if (mx, my) != (0, 0)]
        if not moves:
            blocks += [jnp.zeros((rows, OUTER), BF)] * 3
            continue
        choice = jnp.concatenate([tables[move] for move in moves], axis=0)
        lanes = [slice(3 * line + k, 3 * line + k + 1) for k in range(3)]
        index = jnp.concatenate([place[k, :] for k in lanes], axis=1)
        part = jnp.concatenate([beside[k, :] for k in lanes], axis=1)
        stacked = dot(choice, onehot(TILE, 3 * OUTER, index))
        total = jnp.zeros((rows, 3 * OUTER), F32)
        for k, (mx, my) in enumerate(moves):
            total = jnp.where(part == (mx + 1) * 3 + my + 1, stacked[k * rows : (k + 1) * rows], total)
        total = total.astype(BF)
        blocks += [total[:, k * OUTER : (k + 1) * OUTER] for k in range(3)]
    blocks.append(jnp.zeros((rows, OUTER), BF))
    for q, block in enumerate(blocks):
        far_ref[q * rows : (q + 1) * rows, :] = block
    for g in range(len(blocks) // 4):
        both = jnp.concatenate(blocks[4 * g : 4 * g + 4], axis=0)
        grads = dot(feat_ref[...], both, NT)
        for h in range(2):
            start = (2 * g + h) * rows
            if start < split:
                local = first_ref[start : start + rows, :]
            elif start < cut:
                local = second_ref[start - split : start - split + rows, :]
            else:
                k = 2 * (start - cut)
                local = jnp.concatenate([ahead[k : k + rows], ahead[k + rows : k + 2 * rows]], axis=1)
            sums_ref[start : start + rows, :] = (local + grads[:, h * 128 : (h + 1) * 128]).astype(BF)
    base = len(blocks) // 2 * rows
    sums_ref[base : base + two_ref.shape[0], :] = two_ref[...]
    base = base + two_ref.shape[0]
    sums_ref[base:, :] = jnp.zeros((sums_ref.shape[0] - base, 128), BF)


def sum_kernel(parts_ref, out_ref, *, scale):
    total = jnp.sum(parts_ref[...].astype(F32), axis=0)
    if scale is not None:
        total = total * scale
    total = total.astype(out_ref.dtype)
    for k in range(out_ref.shape[0]):
        out_ref[k] = total


def unpack_kernel(sums_ref, one_ref, two_ref):
    count, rows = one_ref.shape[:2]
    for p in range((count + 1) // 2):
        block = sums_ref[p * rows : (p + 1) * rows, :].astype(F32).T
        for h in range(2):
            if 2 * p + h < count:
                one_ref[count - 1 - 2 * p - h] = block[h * rows : (h + 1) * rows, :]
    base = (count + 1) // 2 * rows
    for k in range(two_ref.shape[0]):
        two_ref[k] = sums_ref[base + k * rows : base + (k + 1) * rows, :].astype(F32)


def finish_kernel(local_ref, far_ref, one_ref, send_ref, out_ref):
    rows, sites = local_ref.shape
    count = one_ref.shape[0]
    weights = jnp.concatenate([one_ref[count - 1 - q] for q in range(count)], axis=0)
    total = dot(weights, far_ref[: count * rows, :], TN)
    first = total.astype(BF)
    rest = total - first.astype(F32)
    second = rest.astype(BF)
    third = (rest - second.astype(F32)).astype(BF)
    spread = dot(jnp.concatenate([first, second, third], axis=0), onehot(sites, OUTER, send_ref[...]), NT)
    spread = spread[:rows] + spread[rows : 2 * rows] + spread[2 * rows :]
    out_ref[...] = (local_ref[...] + spread).astype(BF)


def shift(block, axis, step):
    count = lax.axis_size(axis)
    return lax.ppermute(block, axis, [(i, i + step) for i in range(count) if 0 <= i + step < count])


def around(block):
    three = jnp.concatenate([shift(block, "col", 1), block, shift(block, "col", -1)], axis=0)
    return shift(three, "row", 1), three, shift(three, "row", -1)


def body(
    features, preact, coarse_grad, kernel_one, kernel_two, neighbours, send_list, parent_slot, child_pos
):
    rows, sites = features.shape
    count = neighbours.shape[0]
    wide, owned = coarse_grad.shape
    children = kernel_two.shape[0]
    held = send_list.shape[0]
    n_col, n_row = lax.axis_size("col"), lax.axis_size("row")
    peers = XDIM * n_row
    layers = n_col * n_row // peers
    plane = [[z * peers + i for i in range(peers)] for z in range(layers)]
    tower = [[z * peers + i for z in range(layers)] for i in range(peers)]

    (packed,) = call(pack_kernel, [shape((owned, wide), BF)], [coarse_grad], name="pack")
    coarse = lax.all_to_all(packed.reshape(n_col, owned // n_col, wide), "col", 0, 0, tiled=True)
    coarse = coarse.reshape(owned, wide)

    send = jnp.concatenate([send_list, jnp.full((OUTER - held,), -1, I32)])[None, :]
    near = jnp.concatenate([neighbours, jnp.full((1, sites), sites + 9 * held, I32)], axis=0)
    two_rows = kernel_two.transpose(0, 2, 1).reshape(children * rows, wide)
    pre_grad, pre_out, two_part = call(
        grad_kernel,
        [shape((rows, sites), BF), shape((rows, OUTER), BF), shape((children * rows, wide), BF)],
        [coarse, two_rows, preact, parent_slot[None, :], child_pos[None, :], send],
        flops=2 * 512 * sites * 512,
        name="grads",
    )
    pre_low, pre_mid, pre_high = around(pre_out)

    quads = (count + 3) // 4
    cut = quads - AHEAD
    half = (cut + 1) // 2

    def ahead_body(*refs):
        ahead_kernel(*refs, start=4 * cut)

    ahead, feat_out, near_out = call(
        ahead_body,
        [shape((4 * AHEAD * rows, sites), BF), shape((rows, OUTER), BF), shape((count, OUTER), I32)],
        [features, neighbours, send],
        flops=2 * 256 * sites * 512 * 4 * AHEAD,
        name="ahead",
    )
    halves, local = [], None
    for first, last in ((0, half), (half, cut)):

        def local_body(*refs, first=first, last=last):
            local_kernel(*refs, first=first, last=last)

        part, local = call(
            local_body,
            [shape(((last - first) * 2 * rows, 128), F32), shape((rows, sites), F32)],
            [pre_grad, features, near, kernel_one] + ([] if local is None else [local]),
            flops=2 * 256 * sites * 512 * 4 * (last - first),
            name="local",
        )
        halves.append(part)

    def far_body(*refs):
        far_kernel(*refs, sites=sites, held=held)

    sums, far = call(
        far_body,
        [shape((ROWS, 128), BF), shape(((count + 1) * rows, OUTER), BF)],
        [pre_low, pre_mid, pre_high, near_out, feat_out, pre_grad, ahead, *halves, two_part],
        flops=2 * 256 * OUTER * OUTER * 48,
        name="far",
    )

    share = ROWS // peers
    parts = lax.all_to_all(sums.reshape(peers, share, 128), AXES, 0, 0, axis_index_groups=plane, tiled=True)

    def plane_sum(parts_ref, out_ref):
        sum_kernel(parts_ref, out_ref, scale=None)

    (partial,) = call(plane_sum, [shape((layers, share, 128), BF)], [parts], name="plane_sum")
    parts = lax.all_to_all(partial, AXES, 0, 0, axis_index_groups=tower, tiled=True)
    scale = float(sites * n_col * n_row) ** (-0.5)

    def tower_sum(parts_ref, out_ref):
        sum_kernel(parts_ref, out_ref, scale=scale)

    (whole,) = call(tower_sum, [shape((peers, share, 128), BF)], [parts], name="tower_sum")
    whole = lax.all_to_all(whole, AXES, 0, 0, axis_index_groups=plane, tiled=True)
    one_grad, two_grad = call(
        unpack_kernel,
        [shape((count, rows, rows), F32), shape((children, rows, wide), F32)],
        [whole.reshape(ROWS, 128)],
        name="unpack",
    )

    def late_body(*refs):
        late_kernel(*refs, first=cut, last=quads)

    (local,) = call(
        late_body,
        [shape((rows, sites), F32)],
        [pre_grad, near, kernel_one, local],
        flops=2 * 256 * sites * 512 * 4 * AHEAD,
        name="late",
    )
    (feature_grad,) = call(
        finish_kernel,
        [shape((rows, sites), BF)],
        [local, far, kernel_one, send],
        flops=2 * 256 * OUTER * sites * 4,
        name="finish",
    )
    return feature_grad, one_grad, two_grad.transpose(0, 2, 1)


def solution(mesh):
    placed = (
        P(None, AXES),
        P(None, AXES),
        P(None, AXES),
        P(),
        P(),
        P(None, AXES),
        P(AXES),
        P(AXES),
        P(AXES),
    )
    return jax.shard_map(
        body,
        mesh=mesh,
        in_specs=placed,
        out_specs=(P(None, AXES), P(), P()),
        check_vma=False,
    )
```
